128 devices in a mesh: lon: 16 (over z, y_lo, core), lat: 8 (over x, y_hi).
Axes of the slice: x: 4, y: 4 (y_hi: 2, y_lo: 2; y = y_hi * 2 + y_lo), z: 4, core: 2. Of those that a mesh axis runs over, the one named last changes fastest.
Arguments:
- state: float32 [168, 128, 2048], P(None, 'lat', 'lon'), may hold values from -6 to 6
- noise: float32 [168, 128, 2048], P(None, 'lat', 'lon'), may hold values from -6 to 6
- first_kernel: bfloat16 [9, 256, 168], replicated, may hold values from -0.15625 to 0.15625
- middle_kernels: bfloat16 [2, 9, 256, 256], replicated, may hold values from -0.21875 to 0.21875
- last_kernel: bfloat16 [9, 168, 256], replicated, may hold values from -0.21875 to 0.21875
- obs_values: bfloat16 [12288, 22, 128], P(('lon', 'lat')), may hold values from -6 to 6
- obs_holder: int32 [12288, 1], P(('lon', 'lat')), may hold values from 0 to 127; in each aligned block of 96 rows (0 to 95, 96 to 191, ...) at most 2 rows name the same one
- obs_tile: int32 [12288], P(('lon', 'lat')), may hold values from 0 to 15
- obs_operator: bfloat16 [22, 168], replicated, may hold values from -0.5 to 0.5
- obs_precision: float32 [22], replicated, may hold values from 0.3 to 3
- noise_level: float32 [1], replicated, may hold values from 0.25 to 1
- step_size: float32 [1], replicated, may hold values from 0.05 to 0.2
Outputs:
- state_next: float32 [168, 128, 2048], P(None, 'lat', 'lon')
The draws below stay inside these ranges and needn't reach their ends.
Inputs may be any that keep to these rules, and one draw needn't show every extreme that they name: `obs_holder`: the holder index counts lon-major: lon index times 8 plus lat index; the 96 blocks that one device holds (an aligned block of rows) name one holder at most 2 times, and exactly that often for some holder in every draw.
All inputs are finite; a program needn't handle non-finite values.
Results may differ from the reference program's by a relative error of at most 0.0095.
Values may be sent and summed in bfloat16 or wider, within the bound.
No kernel may reach another device: no remote copies, remote signals or barrier semaphores. Data moves between devices by JAX's collectives and lax.ppermute only.
A program may use at most 128 MiB of HBM per device.

```python
import math
import jax
import jax.numpy as jnp
import numpy as np
from jax import lax

HIDDEN_SIZE = 256
LAYERS = 4
OBS_CHAN = 22
LAT_DEV = 16
LON_DEV = 128
CAPACITY = 2
CHANNELS = 168
BLOCK_DEV = 96
BLOCKS = 12288
GRID_LAT = 128
GRID_LON = 2048
N_LON = 16
N_LAT = 8
DEVICES = 128


def place_ends(values, key, low, high):
    extent = values.shape
    index_at = [jax.random.randint(jax.random.fold_in(key, axis), (), 0, extent[axis]) for axis in range(len(extent))]
    values = values.at[tuple(index_at)].set(low)
    longest = extent.index(max(extent))
    index_at[longest] = (index_at[longest] + 1) % extent[longest]
    return values.at[tuple(index_at)].set(high)


def steps_of(key, extent, cuts, least, top_value):
    level = 1.0
    for axis_at, blocks in cuts:
        draws = jax.random.uniform(jax.random.fold_in(jax.random.fold_in(key, 6), axis_at), (blocks,), jnp.float32, least / len(cuts), top_value / len(cuts))
        level = level * jnp.repeat(jnp.exp(draws), extent[axis_at] // blocks).reshape((-1,) + (1,) * (len(extent) - 1 - axis_at))
    return level


def routed_block(key, own, number, rows, count, top, bound, skew):
    sequence = jax.random.permutation(key, count)
    heavy_load, common = portions_of(count, rows * top, bound, skew, True), portions_of(count, rows * top, bound, skew, False)
    places = jnp.arange(count)

    def named(lengths, rotation):
        used = int((lengths > 0).sum())
        fixed = max(1, used // 4)
        passed = fixed + (places - fixed + rotation * (used - fixed)) % max(1, count - fixed)
        return jnp.zeros((count,), jnp.int32).at[sequence[jnp.where(places < fixed, places, passed)]].set(jnp.asarray(lengths, jnp.int32))

    lengths = jnp.where(number % 4 == 0, named(heavy_load, number // 4), named(common, number - number // 4 - 1))
    mixed = jax.random.permutation(jax.random.fold_in(own, 3), count)
    source_of, taker = mixed[0:count // 2 * 2:2], mixed[1:count // 2 * 2:2]
    slack = jnp.minimum(lengths[source_of] - 1, bound - lengths[taker]) // 2
    slack = jnp.where((source_of == sequence[0]) | (taker == sequence[0]) | (lengths[taker] == 0), 0, jnp.maximum(slack, 0))
    passed = jax.random.randint(jax.random.fold_in(own, 4), (count // 2,), 0, 1 << 20) % (slack + 1)
    lengths = lengths.at[source_of].add(-passed).at[taker].add(passed)
    members = jnp.searchsorted(jnp.cumsum(lengths), jnp.arange(rows * top), side="right").astype(jnp.int32)
    grid = members.reshape(top, rows).T
    grid = grid[jax.random.permutation(jax.random.fold_in(own, 1), rows)]
    rotation = jax.random.randint(jax.random.fold_in(own, 2), (rows, 1), 0, top)
    return jnp.take_along_axis(grid, (jnp.arange(top)[None, :] + rotation) % top, axis=1)


def portions_of(amount, total, reach, lean, full):
    weights = [(1 << 20) // math.isqrt(standing ** lean) + 1 for standing in range(1, amount + 1)]
    largest = reach if full else min(reach, max(-(-total // amount), total * weights[0] // sum(weights)))
    least = 1 if total - largest >= amount - 1 else 0
    holding, surplus = [largest] + [least] * (amount - 1), total - largest - least * (amount - 1)
    while surplus > 0:
        free = [i for i in range(1, amount) if holding[i] < largest] or [i for i in range(1, amount) if holding[i] < reach]
        whole, budget = sum([weights[i] for i in free]), surplus
        for i in free:
            extra = min(reach - holding[i], max(1, budget * weights[i] // whole), surplus)
            holding[i] = holding[i] + extra
            surplus = surplus - extra
    return np.array(holding)


def centred(key, dims, scale, limit, shards=(), kind=jnp.bfloat16):
    values = scale * jax.random.normal(key, dims, jnp.float32)
    if shards:
        values = values * steps_of(key, dims, shards, -0.22, 0.18)
    return jnp.clip(values, -limit, limit).astype(kind)


def setup_inputs(seed: int = 0) -> dict:
    streams_of = jax.random.split(jax.random.key(seed), 13)
    state = centred(streams_of[0], (CHANNELS, GRID_LAT, GRID_LON), 1.0, 6.0, ((1, 8), (2, 16)), jnp.float32)
    noise = centred(streams_of[1], (CHANNELS, GRID_LAT, GRID_LON), 1.0, 6.0, ((1, 8), (2, 16)), jnp.float32)
    first_kernel = centred(streams_of[2], (9, HIDDEN_SIZE, CHANNELS), (9 * CHANNELS) ** -0.5, 0.15625)
    middle_kernels = centred(streams_of[3], (LAYERS - 2, 9, HIDDEN_SIZE, HIDDEN_SIZE), (3 * HIDDEN_SIZE) ** -0.5, 0.21875)
    last_kernel = centred(streams_of[4], (9, CHANNELS, HIDDEN_SIZE), (3 * HIDDEN_SIZE) ** -0.5, 0.21875)
    obs_values = centred(streams_of[5], (BLOCKS, OBS_CHAN, LON_DEV), 1.0, 6.0, ((0, 128),))
    obs_holder_keys = jax.random.split(jax.random.fold_in(streams_of[6], 1), BLOCKS // BLOCK_DEV)
    obs_holder_turns = jax.random.permutation(jax.random.fold_in(streams_of[6], 3), BLOCKS // BLOCK_DEV)
    obs_holder = jax.vmap(lambda own, number: routed_block(jax.random.fold_in(streams_of[6], 2), own, number, BLOCK_DEV, DEVICES, 1, CAPACITY, 2))(obs_holder_keys, obs_holder_turns).reshape((BLOCKS, 1))
    obs_tile = place_ends(jax.random.randint(streams_of[7], (BLOCKS,), 0, LAT_DEV), jax.random.fold_in(streams_of[7], 1), 0, LAT_DEV - 1).astype(jnp.int32)
    obs_operator = centred(streams_of[8], (OBS_CHAN, CHANNELS), CHANNELS ** -0.5, 0.5)
    obs_precision = jnp.clip(jnp.exp(jax.random.uniform(streams_of[9], (OBS_CHAN,), jnp.float32, math.log(0.3), math.log(3.0))), 0.3, 3.0)
    noise_level = jnp.clip(jnp.exp(jax.random.uniform(streams_of[10], (1,), jnp.float32, math.log(0.25), math.log(1.0))), 0.25, 1.0)
    step_size = jnp.clip(jnp.exp(jax.random.uniform(streams_of[11], (1,), jnp.float32, math.log(0.05), math.log(0.2))), 0.05, 0.2)
    return {"state": state, "noise": noise, "first_kernel": first_kernel, "middle_kernels": middle_kernels, "last_kernel": last_kernel, "obs_values": obs_values, "obs_holder": obs_holder, "obs_tile": obs_tile, "obs_operator": obs_operator, "obs_precision": obs_precision, "noise_level": noise_level, "step_size": step_size}


def pad_field(values_in):
    padded = jnp.pad(values_in, ((0, 0), (1, 1), (0, 0)))
    return jnp.concatenate([padded[:, :, -1:], padded, padded[:, :, :1]], axis=2)

def run_conv(padded, taps):
    result = lax.conv_general_dilated(padded.astype(jnp.float32)[None], taps, (1, 1), 'VALID', dimension_numbers=('NCHW', 'OIHW', 'NCHW'), precision=lax.Precision.HIGHEST)
    return result[0]

def forward_conv(padded, kernel):
    taps = kernel.astype(jnp.float32).reshape(3, 3, kernel.shape[1], kernel.shape[2])
    taps = jnp.transpose(taps, (2, 3, 0, 1))
    return run_conv(padded, taps)

def backward_conv(padded, kernel):
    taps = kernel.astype(jnp.float32).reshape(3, 3, kernel.shape[1], kernel.shape[2])
    taps = jnp.transpose(taps, (3, 2, 0, 1))[:, :, ::-1, ::-1]
    return run_conv(padded, taps)

def reference(state, noise, first_kernel, middle_kernels, last_kernel, obs_values, obs_holder, obs_tile, obs_operator, obs_precision, noise_level, step_size):
    kernels = [first_kernel] + [middle_kernels[index] for index in range(LAYERS - 2)] + [last_kernel]
    stored = []
    current = state.astype(jnp.bfloat16)
    for layer in range(LAYERS):
        outputs = forward_conv(pad_field(current), kernels[layer])
        stored.append(outputs)
        if layer + 1 < LAYERS:
            current = jax.nn.silu(outputs).astype(jnp.bfloat16)
    denoised = (state + stored[-1]).astype(jnp.bfloat16)
    holders = obs_holder[:, 0].reshape(DEVICES, BLOCK_DEV)
    tile_rows = obs_tile.reshape(DEVICES, BLOCK_DEV)
    grid_rows = (holders % N_LAT * LAT_DEV + tile_rows).astype(jnp.int32)
    grid_blocks = (holders // N_LAT).astype(jnp.int32)
    values = obs_values.reshape(DEVICES, BLOCK_DEV, OBS_CHAN, LON_DEV)
    blocked = denoised.reshape(CHANNELS, GRID_LAT, N_LON, LON_DEV)
    operator = obs_operator.astype(jnp.float32)

    def one_owner(carry, inputs):
        rows_here, blocks_here, values_here = inputs
        picked = blocked[:, rows_here, blocks_here, :].astype(jnp.float32)
        predicted = jnp.einsum('kc,cbl->bkl', operator, picked)
        weighted = ((values_here.astype(jnp.float32) - predicted) * obs_precision[None, :, None]).astype(jnp.bfloat16)
        contrib = jnp.einsum('kc,bkl->cbl', operator, weighted.astype(jnp.float32))
        return (carry.at[:, rows_here, blocks_here, :].add(contrib), None)
    start = jnp.zeros((CHANNELS, GRID_LAT, N_LON, LON_DEV), jnp.float32)
    pulled, unused = lax.scan(one_owner, start, (grid_rows, grid_blocks, values))
    pulled = pulled.reshape(CHANNELS, GRID_LAT, GRID_LON)
    cotangent = pulled.astype(jnp.bfloat16)
    back = pulled
    for layer in range(LAYERS - 1, -1, -1):
        back = backward_conv(pad_field(cotangent), kernels[layer])
        if layer > 0:
            sigmoid_in = jax.nn.sigmoid(stored[layer - 1])
            cotangent = (back * sigmoid_in * (1.0 + stored[layer - 1] * (1.0 - sigmoid_in))).astype(jnp.bfloat16)
    score = stored[-1] / (noise_level[0] * noise_level[0])
    return state + step_size[0] * (score + pulled + back) + jnp.sqrt(2.0 * step_size[0]) * noise
```

```python
import jax
import jax.numpy as jnp
from jax import lax
from jax.experimental import pallas as pl
from jax.experimental.pallas import tpu as pltpu
from jax.sharding import PartitionSpec as P

LAYERS = 4
CAPACITY = 2
HALO = 4
SIDE = 8
LANES = 256
SLOT = 24
BLOCK = 4
F32 = jnp.float32
BF16 = jnp.bfloat16


def vmem_specs(count):
    return [pl.BlockSpec(memory_space=pltpu.VMEM) for _ in range(count)]


def smem_spec():
    return pl.BlockSpec(memory_space=pltpu.SMEM)


def params():
    return pltpu.CompilerParams(vmem_limit_bytes=60 << 20)


def pack_kernel(slot_ref, tile_ref, values_ref, out_ref, wide_ref):
    channels, count, width = values_ref.shape
    slots = out_ref.shape[0] // SLOT
    onehot = lax.broadcasted_iota(jnp.int32, (slots, count), 0) == slot_ref[...]
    onehot = onehot.astype(F32).astype(BF16)
    for k in range(channels):
        wide_ref[pl.ds(k, slots, stride=SLOT), :] = jnp.dot(
            onehot, values_ref[k], preferred_element_type=F32
        )
    numbers = jnp.broadcast_to((tile_ref[...] + 1).astype(F32), (count, width)).astype(BF16)
    placed = jnp.dot(onehot, numbers, preferred_element_type=F32)
    for k in range(channels, SLOT):
        wide_ref[pl.ds(k, slots, stride=SLOT), :] = placed
    out_ref[...] = wide_ref[...].astype(BF16)


def pack_blocks(slots, tiles, values, slot_count):
    width = values.shape[2]
    return pl.pallas_call(
        pack_kernel,
        out_shape=jax.ShapeDtypeStruct((slot_count * SLOT, width), BF16),
        in_specs=vmem_specs(3),
        out_specs=vmem_specs(1)[0],
        scratch_shapes=[pltpu.VMEM((slot_count * SLOT, width), F32)],
        compiler_params=params(),
        name="pack_blocks",
    )(slots[None, :], tiles[:, None], jnp.transpose(values, (1, 0, 2)))


def put_shifted(dst_ref, row, width, act):
    size = act.shape[0]
    at = pl.ds(row * width, size)
    dst_ref[at, LANES : 2 * LANES] = act.astype(BF16)
    dst_ref[at, 0:LANES] = pltpu.roll(act, 1, 0).astype(BF16)
    dst_ref[at, 2 * LANES : 3 * LANES] = pltpu.roll(act, size - 1, 0).astype(BF16)


def conv_block(src_ref, row, rows, width, w_ref, flip):
    acc = None
    for p in range(3):
        wide = src_ref[pl.ds((row + p) * width, rows * width), :]
        for q in range(3):
            tap = 3 * p + q
            part = jnp.dot(
                wide[:, q * LANES : (q + 1) * LANES],
                w_ref[8 - tap if flip else tap],
                preferred_element_type=F32,
            )
            acc = part if acc is None else acc + part
    return acc


def conv_layer(rows, compute, finish, acc_a, acc_b):
    full, rest = divmod(rows, BLOCK)
    acc_a[...] = compute(0, BLOCK)
    pairs = (full - 1) // 2

    def body(j, carry):
        row = 2 * BLOCK * j
        acc_b[...] = compute(row + BLOCK, BLOCK)
        finish(row, BLOCK, acc_a[...])
        acc_a[...] = compute(row + 2 * BLOCK, BLOCK)
        finish(row + BLOCK, BLOCK, acc_b[...])
        return carry

    lax.fori_loop(0, pairs, body, 0)
    done = 2 * pairs
    if full - 1 > done:
        acc_b[...] = compute((done + 1) * BLOCK, BLOCK)
        finish(done * BLOCK, BLOCK, acc_a[...])
        last = (full - 1, acc_b)
        free = acc_a
    else:
        last = (full - 1, acc_a)
        free = acc_b
    if rest:
        tail = compute(full * BLOCK, rest)
        size = tail.shape[0]
        free[0:size, :] = tail
        finish(last[0] * BLOCK, BLOCK, last[1][...])
        finish(full * BLOCK, rest, free[0:size, :])
    else:
        finish(last[0] * BLOCK, BLOCK, last[1][...])


def forward_kernel(
    band_ref, x_ref, w0, w1, w2, w3, op_ref, pre_ref, pred_ref, d0, d1, d2, buf_a, buf_b, acc_a, acc_b
):
    rows = pre_ref.shape[0]
    width = pre_ref.shape[1]
    cells = width - 2 * SIDE
    weights = (w0, w1, w2, w3)
    slopes = (d0, d1, d2)

    def fill(i, carry):
        part = x_ref[pl.ds(i * 2 * width, 2 * width), :]
        put_shifted(buf_a, i * 2, width, part.astype(F32))
        return carry

    lax.fori_loop(0, (rows + 2 * HALO) // 2, fill, 0)
    src, dst = buf_a, buf_b
    for layer in range(LAYERS):
        margin = HALO - 1 - layer
        count = rows + 2 * margin

        def compute(row, n, src=src, layer=layer):
            return conv_block(src, row, n, width, weights[layer], False)

        if layer < LAYERS - 1:

            def finish(row, n, value, dst=dst, layer=layer):
                gate = 0.5 + 0.5 * jnp.tanh(0.5 * value)
                act = value * gate
                slope = gate + act * (1.0 - gate)
                slopes[layer][pl.ds(row * width, n * width), :] = slope.astype(BF16)
                put_shifted(dst, row, width, act)

        else:

            def finish(row, n, value):
                for i in range(n):
                    part = value[i * width : (i + 1) * width, :]
                    pre_ref[row + i] = part
                    own = x_ref[pl.ds((row + i + HALO) * width, width), :]
                    clean = (own.astype(F32) + part)[SIDE : SIDE + cells, :].astype(BF16)
                    pred_ref[row + i] = lax.dot_general(
                        op_ref[...], clean, (((1,), (1,)), ((), ())), preferred_element_type=F32
                    )

        conv_layer(count, compute, finish, acc_a, acc_b)
        if layer < LAYERS - 1:
            size = margin * width

            def clear(first, dst=dst, layer=layer, size=size):
                slopes[layer][first : first + size, :] = jnp.zeros((size, LANES), BF16)
                dst[first : first + size, :] = jnp.zeros((size, 3 * LANES), BF16)

            @pl.when(band_ref[0] == 0)
            def _():
                clear(0)

            @pl.when(band_ref[0] == band_ref[1] - 1)
            def _(count=count, size=size):
                clear(count * width - size)

        src, dst = dst, src


def forward_pass(band, x, weights, operator, rows, width):
    slope_rows = [rows + 2 * (HALO - 1 - layer) for layer in range(LAYERS - 1)]
    padded = (rows + 2 * HALO) * width
    return pl.pallas_call(
        forward_kernel,
        out_shape=(
            jax.ShapeDtypeStruct((rows, width, LANES), F32),
            jax.ShapeDtypeStruct((rows, operator.shape[0], width - 2 * SIDE), F32),
        )
        + tuple(jax.ShapeDtypeStruct((n * width, LANES), BF16) for n in slope_rows),
        in_specs=[smem_spec()] + vmem_specs(6),
        out_specs=tuple(vmem_specs(5)),
        scratch_shapes=[pltpu.VMEM((padded, 3 * LANES), BF16)] * 2
        + [pltpu.VMEM((BLOCK * width, LANES), F32)] * 2,
        compiler_params=params(),
        name="forward_pass",
    )(band, x, *weights, operator)


def backward_kernel(
    scale_ref, recv_ref, pred_ref, pre_ref, d0, d1, d2, op_ref, prec_ref, w0, w1, w2, w3,
    own_ref, top_ref, bot_ref, wide_ref, sums_ref, buf_a, buf_b, acc_a, acc_b,
):
    rows, width = pre_ref.shape[0], pre_ref.shape[1]
    cells = width - 2 * SIDE
    channels = 22
    slots = recv_ref.shape[0] // SLOT
    lead = HALO + 1
    weights = (w0, w1, w2, w3)
    slopes = (d0, d1, d2)
    zeros = jnp.zeros((4 * width, 3 * LANES), BF16)
    buf_a[width : 5 * width, :] = zeros
    buf_a[(rows + 5) * width : (rows + 9) * width, :] = zeros
    buf_b[0 : 4 * width, :] = zeros
    buf_b[(rows + 6) * width : (rows + 10) * width, :] = zeros

    wide_ref[...] = recv_ref[...].astype(F32)
    sums_ref[...] = jnp.zeros(sums_ref.shape, F32)
    numbers = wide_ref[pl.ds(channels, slots, stride=SLOT), :]
    lane = lax.broadcasted_iota(jnp.int32, (slots, cells), 1).astype(F32) + 1.0
    onehot = jnp.transpose((numbers == lane).astype(F32))[0:rows, :].astype(BF16)
    held = jnp.dot(onehot, jnp.ones((slots, cells), BF16), preferred_element_type=F32)
    for k in range(channels):
        part = wide_ref[pl.ds(k, slots, stride=SLOT), :].astype(BF16)
        sums_ref[pl.ds(k, rows, stride=32), :] = jnp.dot(onehot, part, preferred_element_type=F32)
    for r in range(rows):
        summed = sums_ref[r * 32 : (r + 1) * 32, :]
        weighted = (summed - held[r : r + 1, :] * pred_ref[r]) * prec_ref[...]
        pulled = jnp.dot(
            jnp.transpose(weighted).astype(BF16), op_ref[...], preferred_element_type=F32
        )
        side = jnp.zeros((SIDE, LANES), F32)
        start = pre_ref[r][SIDE : SIDE + cells, :] * scale_ref[0] + pulled
        own_ref[r] = jnp.concatenate([side, start, side], axis=0)
        put_shifted(buf_a, r + lead, width, jnp.concatenate([side, pulled, side], axis=0))

    src, dst = buf_a, buf_b
    for layer in range(LAYERS - 1, -1, -1):
        margin = LAYERS - layer
        count = rows + 2 * margin

        def compute(row, n, src=src, layer=layer, margin=margin):
            return conv_block(src, row + lead - margin - 1, n, width, weights[layer], True)

        if layer > 0:

            def finish(row, n, value, dst=dst, layer=layer, margin=margin):
                slope = slopes[layer - 1][pl.ds(row * width, n * width), :]
                put_shifted(dst, row + lead - margin, width, value * slope.astype(F32))

            conv_layer(count, compute, finish, acc_a, acc_b)
        else:
            top_ref[...] = compute(0, HALO).astype(BF16)
            bot_ref[...] = compute(rows + HALO, HALO).astype(BF16)

            def inner(row, n, src=src, layer=layer, margin=margin):
                return compute(row + HALO, n)

            def finish(row, n, value):
                for i in range(n):
                    own_ref[row + i] = own_ref[row + i] + value[i * width : (i + 1) * width, :]

            conv_layer(rows, inner, finish, acc_a, acc_b)
        src, dst = dst, src


def backward_pass(scale, recv, pred, pre, slopes, operator, precision, weights):
    rows, width = pre.shape[0], pre.shape[1]
    padded = (rows + 2 * (HALO + 1)) * width
    return pl.pallas_call(
        backward_kernel,
        out_shape=(
            jax.ShapeDtypeStruct((rows, width, LANES), F32),
            jax.ShapeDtypeStruct((HALO * width, LANES), BF16),
            jax.ShapeDtypeStruct((HALO * width, LANES), BF16),
        ),
        in_specs=[smem_spec()] + vmem_specs(12),
        out_specs=tuple(vmem_specs(3)),
        scratch_shapes=[
            pltpu.VMEM(recv.shape, F32),
            pltpu.VMEM((rows * 32, recv.shape[1]), F32),
        ]
        + [pltpu.VMEM((padded, 3 * LANES), BF16)] * 2
        + [pltpu.VMEM((BLOCK * width, LANES), F32)] * 2,
        compiler_params=params(),
        name="backward_pass",
    )(scale, recv, pred, pre, *slopes, operator, precision, *weights)


def final_kernel(
    scale_ref, own_ref, above_ref, below_ref, left_ref, right_ref, state_ref, noise_ref, out_ref
):
    rows, width = own_ref.shape[0], own_ref.shape[1]
    cells = width - 2 * SIDE
    channels = state_ref.shape[0]
    for r in range(rows):
        total = own_ref[r][SIDE : SIDE + cells, :]
        if r < HALO:
            total = total + above_ref[r * width : (r + 1) * width, :].astype(F32)[SIDE : SIDE + cells, :]
        if r >= rows - HALO:
            at = r - (rows - HALO)
            total = total + below_ref[at * width : (at + 1) * width, :].astype(F32)[SIDE : SIDE + cells, :]
        first = total[0:SIDE, :] + left_ref[r]
        last = total[cells - SIDE : cells, :] + right_ref[r]
        total = jnp.concatenate([first, total[SIDE : cells - SIDE, :], last], axis=0)
        turned = jnp.transpose(total)[0:channels, :]
        out_ref[:, r, :] = (
            state_ref[:, r, :] + scale_ref[0] * turned + scale_ref[1] * noise_ref[:, r, :]
        )


def final_pass(scale, own, above, below, left, right, state, noise):
    return pl.pallas_call(
        final_kernel,
        out_shape=jax.ShapeDtypeStruct(state.shape, F32),
        in_specs=[smem_spec()] + vmem_specs(7),
        out_specs=vmem_specs(1)[0],
        compiler_params=params(),
        name="final_pass",
    )(scale, own, above, below, left, right, state, noise)


def swap_pairs(size, first, wrap):
    pairs = []
    for low in range(first, size if wrap else size - 1, 2):
        high = (low + 1) % size
        pairs += [(low, high), (high, low)]
    return pairs


def exchange(axis, wrap, to_before, to_after):
    size = lax.axis_size(axis)
    even = lax.axis_index(axis) % 2 == 0
    near = lax.ppermute(jnp.where(even, to_after, to_before), axis, swap_pairs(size, 0, wrap))
    far = lax.ppermute(jnp.where(even, to_before, to_after), axis, swap_pairs(size, 1, wrap))
    return jnp.where(even, far, near), jnp.where(even, near, far)


def pad_to(values, shape):
    return jnp.pad(values, [(0, n - m) for m, n in zip(values.shape, shape)])


def shards(
    state,
    noise,
    first_kernel,
    middle_kernels,
    last_kernel,
    obs_values,
    obs_holder,
    obs_tile,
    obs_operator,
    obs_precision,
    noise_level,
    step_size,
):
    channels, rows, cells = state.shape
    width = cells + 2 * SIDE
    square = (9, LANES, LANES)
    kernels = [pad_to(first_kernel, square), middle_kernels[0], middle_kernels[1], pad_to(last_kernel, square)]
    turned = [jnp.transpose(kernel, (0, 2, 1)) for kernel in kernels]

    targets = obs_holder[:, 0]
    count = targets.shape[0]
    positions = lax.broadcasted_iota(jnp.int32, (count, count), 0)
    earlier = lax.broadcasted_iota(jnp.int32, (count, count), 1)
    before = (targets[:, None] == targets[None, :]) & (earlier < positions)
    slots = targets * CAPACITY + jnp.sum(before.astype(jnp.int32), axis=1)
    holders = lax.axis_size(("lon", "lat"))
    packed = pack_blocks(slots, obs_tile, obs_values, holders * CAPACITY)
    recv = lax.all_to_all(
        packed.reshape(holders, CAPACITY * SLOT, cells), ("lon", "lat"), split_axis=0, concat_axis=0, tiled=True
    ).reshape(packed.shape)

    x = jnp.transpose(state.astype(BF16), (1, 2, 0))
    x = pad_to(x, (rows, cells, LANES))
    left, right = exchange("lon", True, x[:, :SIDE], x[:, cells - SIDE :])
    x = jnp.concatenate([left, x, right], axis=1)
    above, below = exchange("lat", False, x[:HALO], x[rows - HALO :])
    x = jnp.concatenate([above, x, below], axis=0).reshape(-1, LANES)

    band = jnp.stack([lax.axis_index("lat"), lax.axis_size("lat")]).astype(jnp.int32)
    operator = pad_to(obs_operator, (32, LANES))
    precision = pad_to(obs_precision[:, None], (32, 1))
    pre, pred, *slopes = forward_pass(band, x, turned, operator, rows, width)
    inverse = (1.0 / (noise_level * noise_level)).astype(F32)
    own, top, bottom = backward_pass(inverse, recv, pred, pre, slopes, operator, precision, kernels)
    above, below = exchange("lat", False, top, bottom)
    above_side = above.reshape(HALO, width, LANES)
    below_side = below.reshape(HALO, width, LANES)

    def edge(at):
        added = [
            above_side[:, at : at + SIDE].astype(F32),
            jnp.zeros((rows - 2 * HALO, SIDE, LANES), F32),
            below_side[:, at : at + SIDE].astype(F32),
        ]
        return (own[:, at : at + SIDE] + jnp.concatenate(added, axis=0)).astype(BF16)

    left, right = exchange("lon", True, edge(0), edge(width - SIDE))
    scale = jnp.stack([step_size[0], jnp.sqrt(2.0 * step_size[0])])
    return final_pass(scale, own, above, below, left.astype(F32), right.astype(F32), state, noise)


def solution(mesh):
    placed = (
        P(None, "lat", "lon"),
        P(None, "lat", "lon"),
        P(),
        P(),
        P(),
        P(("lon", "lat"), None, None),
        P(("lon", "lat"), None),
        P(("lon", "lat")),
        P(),
        P(),
        P(),
        P(),
    )
    return jax.shard_map(
        shards, mesh=mesh, in_specs=placed, out_specs=P(None, "lat", "lon"), check_vma=False
    )
```

```python
import jax
import jax.numpy as jnp
from jax import lax
from jax.experimental import pallas as pl
from jax.experimental.pallas import tpu as pltpu
from jax.sharding import PartitionSpec as P


LAYERS = 4
CAPACITY = 2
HALO = 4
SIDE = 8
LANES = 256
SLOT = 24
BLOCK = 4
F32 = jnp.float32
BF16 = jnp.bfloat16


def vmem_specs(count):
    return [pl.BlockSpec(memory_space=pltpu.VMEM) for _ in range(count)]


def smem_spec():
    return pl.BlockSpec(memory_space=pltpu.SMEM)


def params(mebibytes):
    return pltpu.CompilerParams(vmem_limit_bytes=mebibytes << 20)


def near_core(*arrays):
    return [pltpu.with_memory_space_constraint(array, pltpu.VMEM) for array in arrays]


def in_hbm(*arrays):
    return [pltpu.with_memory_space_constraint(array, pltpu.HBM) for array in arrays]


def far_specs(count):
    return [pl.BlockSpec(memory_space=pl.ANY) for _ in range(count)]


def copies(pairs, sems):
    return [pltpu.make_async_copy(src, dst, sems.at[i]) for i, (src, dst) in enumerate(pairs)]


def pack_kernel(slot_ref, tile_ref, values_ref, out_ref, wide_ref):
    channels, count, width = values_ref.shape
    slots = out_ref.shape[0] // SLOT
    onehot = lax.broadcasted_iota(jnp.int32, (slots, count), 0) == slot_ref[...]
    onehot = onehot.astype(F32).astype(BF16)
    for k in range(channels):
        wide_ref[pl.ds(k, slots, stride=SLOT), :] = jnp.dot(
            onehot, values_ref[k], preferred_element_type=F32
        )
    numbers = jnp.broadcast_to((tile_ref[...] + 1).astype(F32), (count, width)).astype(BF16)
    placed = jnp.dot(onehot, numbers, preferred_element_type=F32)
    for k in range(channels, SLOT):
        wide_ref[pl.ds(k, slots, stride=SLOT), :] = placed
    out_ref[...] = wide_ref[...].astype(BF16)


def pack_blocks(slots, tiles, values, slot_count):
    width = values.shape[2]
    return pl.pallas_call(
        pack_kernel,
        out_shape=jax.ShapeDtypeStruct((slot_count * SLOT, width), BF16),
        in_specs=vmem_specs(3),
        out_specs=vmem_specs(1)[0],
        scratch_shapes=[pltpu.VMEM((slot_count * SLOT, width), F32)],
        compiler_params=params(12),
        name="pack_blocks",
    )(slots[None, :], tiles[:, None], jnp.transpose(values, (1, 0, 2)))


def put_shifted(dst_ref, row, width, act):
    size, channels = act.shape
    at = pl.ds(row * width, size)
    dst_ref[at, LANES : LANES + channels] = act.astype(BF16)
    dst_ref[at, 0:channels] = pltpu.roll(act, 1, 0).astype(BF16)
    dst_ref[at, 2 * LANES : 2 * LANES + channels] = pltpu.roll(act, size - 1, 0).astype(BF16)


def conv_block(src_ref, row, rows, width, w_ref, side, flip):
    acc = None
    taken = w_ref.shape[1 + side]
    for p in range(3):
        at = pl.ds((row + p) * width, rows * width)
        for q in range(3):
            tap = 3 * p + q
            part = lax.dot_general(
                src_ref[at, q * LANES : q * LANES + taken],
                w_ref[8 - tap if flip else tap],
                (((1,), (side,)), ((), ())),
                preferred_element_type=F32,
            )
            acc = part if acc is None else acc + part
    return acc


def conv_layer(rows, compute, finish, acc_a, acc_b):
    full, rest = divmod(rows, BLOCK)
    first = compute(0, BLOCK)
    size, channels = first.shape
    unit = size // BLOCK

    def keep(acc, value):
        acc[0 : value.shape[0], 0:channels] = value

    def kept(acc, n):
        return acc[0 : n * unit, 0:channels]

    keep(acc_a, first)
    pairs = (full - 1) // 2

    def body(j, carry):
        row = 2 * BLOCK * j
        keep(acc_b, compute(row + BLOCK, BLOCK))
        finish(row, BLOCK, kept(acc_a, BLOCK))
        keep(acc_a, compute(row + 2 * BLOCK, BLOCK))
        finish(row + BLOCK, BLOCK, kept(acc_b, BLOCK))
        return carry

    lax.fori_loop(0, pairs, body, 0)
    done = 2 * pairs
    last, free = acc_a, acc_b
    if full - 1 > done:
        keep(acc_b, compute((done + 1) * BLOCK, BLOCK))
        finish(done * BLOCK, BLOCK, kept(acc_a, BLOCK))
        last, free = acc_b, acc_a
    if rest:
        keep(free, compute(full * BLOCK, rest))
    finish((full - 1) * BLOCK, BLOCK, kept(last, BLOCK))
    if rest:
        finish(full * BLOCK, rest, kept(free, rest))


def either(flag, yes, no):
    return jnp.where(flag == 1, yes, no)


def turn_kernel(place_ref, state_ref, own_ref, near_ref, far_ref, low_ref, high_ref):
    _, rows, cells = state_ref.shape
    for r in range(rows):
        part = jnp.transpose(state_ref[:, r, :])
        own_ref[r * cells : (r + 1) * cells, :] = part.astype(BF16)
        low_ref[r * SIDE : (r + 1) * SIDE, :] = part[0:SIDE, :]
        high_ref[r * SIDE : (r + 1) * SIDE, :] = part[cells - SIDE : cells, :]
    low = low_ref[...]
    high = high_ref[...]
    near_ref[...] = either(place_ref[0], high, low).astype(BF16)
    far_ref[...] = either(place_ref[0], low, high).astype(BF16)


def turn_state(place, state):
    channels, rows, cells = state.shape
    edge = (rows * SIDE, channels)
    return pl.pallas_call(
        turn_kernel,
        out_shape=(
            pltpu.HBM((rows * cells, channels), BF16),
            jax.ShapeDtypeStruct(edge, BF16),
            jax.ShapeDtypeStruct(edge, BF16),
        ),
        in_specs=[smem_spec()] + vmem_specs(1),
        out_specs=tuple(vmem_specs(3)),
        scratch_shapes=[pltpu.VMEM(edge, F32)] * 2,
        compiler_params=params(8),
        name="turn_state",
    )(place, *near_core(state))


def framed_row(place_ref, own_ref, near_ref, far_ref, r, cells):
    at = pl.ds(r * SIDE, SIDE)
    near = near_ref[at, :].astype(F32)
    far = far_ref[at, :].astype(F32)
    own = own_ref[pl.ds(r * cells, cells), :].astype(F32)
    left = either(place_ref[0], far, near)
    right = either(place_ref[0], near, far)
    return jnp.concatenate([left, own, right], axis=0)


def frame_kernel(place_ref, own_ref, lon_near_ref, lon_far_ref, near_ref, far_ref):
    rows = lon_near_ref.shape[0] // SIDE
    cells = own_ref.shape[0] // rows
    width = cells + 2 * SIDE
    for i in range(HALO):
        top = framed_row(place_ref, own_ref, lon_near_ref, lon_far_ref, i, cells)
        low = framed_row(place_ref, own_ref, lon_near_ref, lon_far_ref, rows - HALO + i, cells)
        at = pl.ds(i * width, width)
        near_ref[at, :] = either(place_ref[1], low, top).astype(BF16)
        far_ref[at, :] = either(place_ref[1], top, low).astype(BF16)


def frame_rows(place, own, lon_near, lon_far, width):
    shape = (HALO * width, own.shape[1])
    return pl.pallas_call(
        frame_kernel,
        out_shape=(jax.ShapeDtypeStruct(shape, BF16),) * 2,
        in_specs=[smem_spec()] + vmem_specs(3),
        out_specs=tuple(vmem_specs(2)),
        compiler_params=params(8),
        name="frame_rows",
    )(place, *in_hbm(own), lon_near, lon_far)


def weight_scratch(weights):
    return [pltpu.VMEM(weight.shape, BF16) for weight in weights]


def forward_kernel(
    place_ref, own_ref, lon_near_ref, lon_far_ref, lat_near_ref, lat_far_ref, op_ref, w0_far, wm_far, w3_far,
    pre_far, pred_ref, d0_far, d1_far, d2_far,
    buf_a, buf_b, acc_a, acc_b, w0, wm, w3, pre_ref, d0, d1, d2, in_sems, out_sems,
):
    rows, width, _ = pre_ref.shape
    cells = width - 2 * SIDE
    weights = (w0, wm.at[0], wm.at[1], w3)
    slopes = (d0, d1, d2)
    loads = copies(
        ((w0_far, w0), (wm_far.at[0], wm.at[0]), (wm_far.at[1], wm.at[1]), (w3_far, w3)), in_sems
    )
    stores = copies(((d0, d0_far), (d1, d1_far), (d2, d2_far), (pre_ref, pre_far)), out_sems)
    for load in loads:
        load.start()

    def fill(i, carry):
        put_shifted(buf_a, i + HALO, width, framed_row(place_ref, own_ref, lon_near_ref, lon_far_ref, i, cells))
        return carry

    lax.fori_loop(0, rows, fill, 0)
    for i in range(HALO):
        at = pl.ds(i * width, width)
        near = lat_near_ref[at, :].astype(F32)
        far = lat_far_ref[at, :].astype(F32)
        put_shifted(buf_a, i, width, either(place_ref[1], far, near))
        put_shifted(buf_a, i + HALO + rows, width, either(place_ref[1], near, far))
    src, dst = buf_a, buf_b
    for layer in range(LAYERS):
        margin = HALO - 1 - layer
        count = rows + 2 * margin

        def compute(row, n, src=src, layer=layer):
            return conv_block(src, row, n, width, weights[layer], 0 if layer == 0 else 1, False)

        loads[layer].wait()

        if layer < LAYERS - 1:

            def finish(row, n, value, dst=dst, layer=layer):
                gate = 0.5 + 0.5 * jnp.tanh(0.5 * value)
                act = value * gate
                slope = gate + act * (1.0 - gate)
                slopes[layer][pl.ds(row * width, n * width), :] = slope.astype(BF16)
                put_shifted(dst, row, width, act)

        else:

            def finish(row, n, value):
                for i in range(n):
                    part = value[i * width : (i + 1) * width, :]
                    pre_ref[row + i] = part
                    own = own_ref[pl.ds((row + i) * cells, cells), :].astype(F32)
                    clean = (own + part[SIDE : SIDE + cells, :]).astype(BF16)
                    pred_ref[row + i] = lax.dot_general(
                        op_ref[...], clean, (((1,), (1,)), ((), ())), preferred_element_type=F32
                    )

        conv_layer(count, compute, finish, acc_a, acc_b)
        if layer < LAYERS - 1:
            size = margin * width

            def clear(first, dst=dst, layer=layer, size=size):
                slopes[layer][first : first + size, :] = jnp.zeros((size, LANES), BF16)
                dst[first : first + size, :] = jnp.zeros((size, 3 * LANES), BF16)

            @pl.when(place_ref[2] == 1)
            def _():
                clear(0)

            @pl.when(place_ref[3] == 1)
            def _(count=count, size=size):
                clear(count * width - size)

        stores[layer].start()
        src, dst = dst, src
    for store in stores:
        store.wait()


def forward_pass(place, own, lon, lat, weights, operator, rows, width):
    slopes = [((rows + 2 * (HALO - 1 - layer)) * width, LANES) for layer in range(LAYERS - 1)]
    pre = (rows, width, own.shape[1])
    padded = (rows + 2 * HALO) * width
    return pl.pallas_call(
        forward_kernel,
        out_shape=(
            pltpu.HBM(pre, F32),
            pltpu.HBM((rows, operator.shape[0], width - 2 * SIDE), F32),
        )
        + tuple(pltpu.HBM(shape, BF16) for shape in slopes),
        in_specs=[smem_spec()] + vmem_specs(6) + far_specs(3),
        out_specs=tuple(far_specs(1) + vmem_specs(1) + far_specs(3)),
        scratch_shapes=[pltpu.VMEM((padded, 3 * LANES), BF16)] * 2
        + [pltpu.VMEM((BLOCK * width, LANES), F32)] * 2
        + weight_scratch(weights)
        + [pltpu.VMEM(pre, F32)]
        + [pltpu.VMEM(shape, BF16) for shape in slopes]
        + [pltpu.SemaphoreType.DMA((LAYERS,)), pltpu.SemaphoreType.DMA((LAYERS,))],
        compiler_params=params(34),
        name="forward_pass",
    )(place, *in_hbm(own), *lon, *lat, operator, *in_hbm(*weights))


LEAD = HALO + 1


def slope_rows(layer, first):
    return first - (layer - HALO + 1)


def edge_kernel(
    place_ref, recv_ref, pred_ref, op_ref, prec_ref, d0_far, d1_far, d2_far, w0_far, wm_far, w3_far,
    pulled_ref, near_ref, far_ref, s0_ref, s1_ref, s2_ref,
    wide_ref, sums_ref, buf_a, buf_b, acc_a, acc_b, w0, wm, w3, d_ref, in_sems,
):
    rows, cells, channels = pulled_ref.shape
    width = cells + 2 * SIDE
    bands = 22
    slots = recv_ref.shape[0] // SLOT
    weights = (w0, wm.at[0], wm.at[1], w3)
    strips = (s0_ref, s1_ref, s2_ref)
    size = HALO * width
    pairs = [(w3_far, w3), (wm_far.at[1], wm.at[1]), (wm_far.at[0], wm.at[0]), (w0_far, w0)]
    for layer, source in ((2, d2_far), (1, d1_far), (0, d0_far)):
        for end in range(2):
            first = layer + 1 - HALO if end == 0 else rows - 1 - layer
            at = slope_rows(layer, first) * width
            pairs.append((source.at[pl.ds(at, size)], d_ref.at[layer, end]))
    loads = copies(pairs, in_sems)
    for load in loads:
        load.start()

    nothing = jnp.zeros((4 * width, 3 * LANES), BF16)
    buf_a[width : 5 * width, :] = nothing
    buf_a[(rows + 5) * width : (rows + 9) * width, :] = nothing
    buf_b[0 : 4 * width, :] = nothing
    buf_b[(rows + 6) * width : (rows + 10) * width, :] = nothing

    wide_ref[...] = recv_ref[...].astype(F32)
    sums_ref[...] = jnp.zeros(sums_ref.shape, F32)
    numbers = wide_ref[pl.ds(bands, slots, stride=SLOT), :]
    lane = lax.broadcasted_iota(jnp.int32, (slots, cells), 1).astype(F32) + 1.0
    onehot = jnp.transpose((numbers == lane).astype(F32))[0:rows, :].astype(BF16)
    held = jnp.dot(onehot, jnp.ones((slots, cells), BF16), preferred_element_type=F32)
    for k in range(bands):
        part = wide_ref[pl.ds(k, slots, stride=SLOT), :].astype(BF16)
        sums_ref[pl.ds(k, rows, stride=32), :] = jnp.dot(onehot, part, preferred_element_type=F32)
    for r in range(rows):
        summed = sums_ref[r * 32 : (r + 1) * 32, :]
        weighted = (summed - held[r : r + 1, :] * pred_ref[r]) * prec_ref[...]
        pulled = jnp.dot(
            jnp.transpose(weighted).astype(BF16), op_ref[...], preferred_element_type=F32
        )
        pulled_ref[r] = pulled
        if r < HALO or r >= rows - HALO:
            side = jnp.zeros((SIDE, channels), F32)
            put_shifted(buf_a, r + LEAD, width, jnp.concatenate([side, pulled, side], axis=0))

    src, dst = buf_a, buf_b
    for layer in range(LAYERS - 1, -1, -1):
        margin = LAYERS - layer
        tops = (-margin, rows + margin - HALO)
        accs = (acc_a, acc_b)
        loads[LAYERS - 1 - layer].wait()
        for end in range(2):
            value = conv_block(
                src, tops[end] + LEAD - 1, HALO, width, weights[layer], 1 if layer == 0 else 0, True
            )
            accs[end][:, 0 : value.shape[1]] = value
        if layer > 0:
            for end in range(2):
                loads[LAYERS + 2 * (LAYERS - 1 - layer) + end].wait()
                value = accs[end][...] * d_ref[layer - 1, end].astype(F32)
                put_shifted(dst, tops[end] + LEAD, width, value)
                half = size // 2
                kept = value[half:, :] if end == 0 else value[0:half, :]
                strips[layer - 1][end * half : (end + 1) * half, :] = kept.astype(BF16)
        else:
            top = acc_a[:, 0:channels]
            low = acc_b[:, 0:channels]
            near_ref[...] = either(place_ref[1], low, top).astype(BF16)
            far_ref[...] = either(place_ref[1], top, low).astype(BF16)
        src, dst = dst, src


def edge_pass(place, recv, pred, slopes, operator, precision, weights, channels):
    rows, cells = pred.shape[0], pred.shape[2]
    width = cells + 2 * SIDE
    padded = (rows + 2 * LEAD) * width
    size = HALO * width
    return pl.pallas_call(
        edge_kernel,
        out_shape=(
            pltpu.HBM((rows, cells, channels), F32),
            jax.ShapeDtypeStruct((size, channels), BF16),
            jax.ShapeDtypeStruct((size, channels), BF16),
        )
        + tuple(pltpu.HBM((size, LANES), BF16) for _ in range(LAYERS - 1)),
        in_specs=[smem_spec()] + vmem_specs(4) + far_specs(6),
        out_specs=tuple(vmem_specs(6)),
        scratch_shapes=[
            pltpu.VMEM(recv.shape, F32),
            pltpu.VMEM((rows * 32, recv.shape[1]), F32),
        ]
        + [pltpu.VMEM((padded, 3 * LANES), BF16)] * 2
        + [pltpu.VMEM((size, LANES), F32)] * 2
        + weight_scratch(weights)
        + [pltpu.VMEM((LAYERS - 1, 2, size, LANES), BF16), pltpu.SemaphoreType.DMA((LAYERS + 6,))],
        compiler_params=params(34),
        name="edge_pass",
    )(place, recv, *in_hbm(pred), operator, precision, *in_hbm(*slopes, *weights))


def inner_kernel(
    scale_ref, pulled_ref, s0_ref, s1_ref, s2_ref, pre_far, d0_far, d1_far, d2_far, w0_far, wm_far, w3_far,
    own_ref,
    buf_a, buf_b, acc_a, acc_b, w0, wm, w3, pre_ref, d0, d1, d2, in_sems,
):
    rows, cells, channels = pulled_ref.shape
    width = cells + 2 * SIDE
    weights = (w0, wm.at[0], wm.at[1], w3)
    strips = (s0_ref, s1_ref, s2_ref)
    slopes = (d0, d1, d2)
    pairs = [(w3_far, w3)]
    for layer, source, weight in ((2, d2_far, 1), (1, d1_far, 0), (0, d0_far, None)):
        first = layer + 1
        count = slopes[layer].shape[0]
        pairs.append((source.at[pl.ds(slope_rows(layer, first) * width, count)], slopes[layer]))
        pairs.append((w0_far, w0) if weight is None else (wm_far.at[weight], wm.at[weight]))
    pairs.append((pre_far, pre_ref))
    loads = copies(pairs, in_sems)
    for load in loads:
        load.start()

    def fill(r, carry):
        side = jnp.zeros((SIDE, channels), F32)
        put_shifted(buf_a, r + LEAD, width, jnp.concatenate([side, pulled_ref[r], side], axis=0))
        return carry

    lax.fori_loop(0, rows, fill, 0)
    loads[0].wait()
    src, dst = buf_a, buf_b
    half = HALO // 2 * width
    for layer in range(LAYERS - 1, -1, -1):
        begin = layer
        count = rows - 2 * layer

        def compute(row, n, src=src, layer=layer, begin=begin):
            return conv_block(
                src, row + begin + LEAD - 1, n, width, weights[layer], 1 if layer == 0 else 0, True
            )

        if layer > 0:
            kept = strips[layer - 1]
            put_shifted(dst, layer - 2 + LEAD, width, kept[0:half, :].astype(F32))
            put_shifted(dst, rows - layer + LEAD, width, kept[half:, :].astype(F32))
            loads[2 * (LAYERS - 1 - layer) + 1].wait()

            def finish(row, n, value, dst=dst, layer=layer, begin=begin):
                slope = slopes[layer - 1][pl.ds(row * width, n * width), :]
                put_shifted(dst, row + begin + LEAD, width, value * slope.astype(F32))

            conv_layer(count, compute, finish, acc_a, acc_b)
            loads[2 * (LAYERS - 1 - layer) + 2].wait()
        else:
            loads[-1].wait()

            def finish(row, n, value):
                side = jnp.zeros((SIDE, channels), F32)
                for i in range(n):
                    base = pre_ref[row + i][SIDE : SIDE + cells, :] * scale_ref[0] + pulled_ref[row + i]
                    base = jnp.concatenate([side, base, side], axis=0)
                    own_ref[row + i] = base + value[i * width : (i + 1) * width, :]

            conv_layer(count, compute, finish, acc_a, acc_b)
        src, dst = dst, src


def inner_pass(scale, pulled, strips, pre, slopes, weights):
    rows, width, channels = pre.shape
    padded = (rows + 2 * LEAD) * width
    kept = [((rows - 2 * (layer + 1)) * width, LANES) for layer in range(LAYERS - 1)]
    return pl.pallas_call(
        inner_kernel,
        out_shape=pltpu.HBM((rows, width, channels), F32),
        in_specs=[smem_spec()] + vmem_specs(4) + far_specs(7),
        out_specs=vmem_specs(1)[0],
        scratch_shapes=[pltpu.VMEM((padded, 3 * LANES), BF16)] * 2
        + [pltpu.VMEM((BLOCK * width, LANES), F32)] * 2
        + weight_scratch(weights)
        + [pltpu.VMEM(pre.shape, F32)]
        + [pltpu.VMEM(shape, BF16) for shape in kept]
        + [pltpu.SemaphoreType.DMA((2 * LAYERS,))],
        compiler_params=params(34),
        name="inner_pass",
    )(scale, *in_hbm(pulled, *strips, pre, *slopes, *weights))


def final_kernel(
    scale_ref, own_ref, above_ref, below_ref, left_ref, right_ref, state_ref, noise_ref, out_ref
):
    rows, width = own_ref.shape[0], own_ref.shape[1]
    cells = width - 2 * SIDE
    for r in range(rows):
        total = own_ref[r][SIDE : SIDE + cells, :]
        if r < HALO:
            total = total + above_ref[r * width : (r + 1) * width, :].astype(F32)[SIDE : SIDE + cells, :]
        if r >= rows - HALO:
            at = r - (rows - HALO)
            total = total + below_ref[at * width : (at + 1) * width, :].astype(F32)[SIDE : SIDE + cells, :]
        first = total[0:SIDE, :] + left_ref[r]
        last = total[cells - SIDE : cells, :] + right_ref[r]
        total = jnp.concatenate([first, total[SIDE : cells - SIDE, :], last], axis=0)
        turned = jnp.transpose(total)
        out_ref[:, r, :] = (
            state_ref[:, r, :] + scale_ref[0] * turned + scale_ref[1] * noise_ref[:, r, :]
        )


def final_pass(scale, own, above, below, left, right, state, noise):
    return pl.pallas_call(
        final_kernel,
        out_shape=jax.ShapeDtypeStruct(state.shape, F32),
        in_specs=[smem_spec()] + vmem_specs(7),
        out_specs=vmem_specs(1)[0],
        compiler_params=params(16),
        name="final_pass",
    )(scale, *in_hbm(own), above, below, left, right, *near_core(state, noise))


def swap_pairs(size, first, wrap):
    pairs = []
    for low in range(first, size if wrap else size - 1, 2):
        high = (low + 1) % size
        pairs += [(low, high), (high, low)]
    return pairs


def swap(axis, wrap, near, far):
    size = lax.axis_size(axis)
    return lax.ppermute(near, axis, swap_pairs(size, 0, wrap)), lax.ppermute(far, axis, swap_pairs(size, 1, wrap))


def exchange(axis, wrap, to_before, to_after):
    even = lax.axis_index(axis) % 2 == 0
    near, far = swap(axis, wrap, jnp.where(even, to_after, to_before), jnp.where(even, to_before, to_after))
    return jnp.where(even, far, near), jnp.where(even, near, far)


def pad_to(values, shape):
    return jnp.pad(values, [(0, n - m) for m, n in zip(values.shape, shape)])


def shards(
    state,
    noise,
    first_kernel,
    middle_kernels,
    last_kernel,
    obs_values,
    obs_holder,
    obs_tile,
    obs_operator,
    obs_precision,
    noise_level,
    step_size,
):
    channels, rows, cells = state.shape
    width = cells + 2 * SIDE
    weights = (jnp.transpose(first_kernel, (0, 2, 1)), middle_kernels, last_kernel)
    lon, lat = lax.axis_index("lon"), lax.axis_index("lat")
    bands = lax.axis_size("lat")
    place = jnp.stack([lon % 2 == 0, lat % 2 == 0, lat == 0, lat == bands - 1]).astype(jnp.int32)

    targets = obs_holder[:, 0]
    count = targets.shape[0]
    positions = lax.broadcasted_iota(jnp.int32, (count, count), 0)
    earlier = lax.broadcasted_iota(jnp.int32, (count, count), 1)
    before = (targets[:, None] == targets[None, :]) & (earlier < positions)
    slots = targets * CAPACITY + jnp.sum(before.astype(jnp.int32), axis=1)
    holders = lax.axis_size(("lon", "lat"))
    packed = pack_blocks(slots, obs_tile, obs_values, holders * CAPACITY)
    own, *edges = turn_state(place, state)
    lon_halo = swap("lon", True, *edges)
    framed = frame_rows(place, own, *lon_halo, width)
    packed, framed = lax.optimization_barrier((packed, framed))
    lat_halo = swap("lat", False, *framed)
    recv = lax.all_to_all(
        packed.reshape(holders, CAPACITY * SLOT, cells), ("lon", "lat"), split_axis=0, concat_axis=0, tiled=True
    ).reshape(packed.shape)

    operator = pad_to(obs_operator, (32, channels))
    precision = pad_to(obs_precision[:, None], (32, 1))
    pre, pred, *slopes = forward_pass(place, own, lon_halo, lat_halo, weights, operator, rows, width)
    inverse = (1.0 / (noise_level * noise_level)).astype(F32)
    pulled, near, far, *strips = edge_pass(
        place, recv, pred, slopes, operator, precision, weights, channels
    )
    near, far = swap("lat", False, near, far)
    own = inner_pass(inverse, pulled, strips, pre, slopes, weights)
    even = place[1] == 1
    above, below = jnp.where(even, far, near), jnp.where(even, near, far)
    above_side = above.reshape(HALO, width, channels)
    below_side = below.reshape(HALO, width, channels)

    def edge(at):
        added = [
            above_side[:, at : at + SIDE].astype(F32),
            jnp.zeros((rows - 2 * HALO, SIDE, channels), F32),
            below_side[:, at : at + SIDE].astype(F32),
        ]
        return (own[:, at : at + SIDE] + jnp.concatenate(added, axis=0)).astype(BF16)

    left, right = exchange("lon", True, edge(0), edge(width - SIDE))
    scale = jnp.stack([step_size[0], jnp.sqrt(2.0 * step_size[0])])
    return final_pass(scale, own, above, below, left.astype(F32), right.astype(F32), state, noise)


def solution(mesh):
    placed = (
        P(None, "lat", "lon"),
        P(None, "lat", "lon"),
        P(),
        P(),
        P(),
        P(("lon", "lat"), None, None),
        P(("lon", "lat"), None),
        P(("lon", "lat")),
        P(),
        P(),
        P(),
        P(),
    )

    return jax.shard_map(
        shards, mesh=mesh, in_specs=placed, out_specs=P(None, "lat", "lon"), check_vma=False
    )
```

```python
import functools

import jax
import jax.numpy as jnp
from jax import lax
from jax.experimental import pallas as pl
from jax.experimental.pallas import tpu as pltpu
from jax.sharding import PartitionSpec as P


LAYERS = 4
CAPACITY = 2
HALO = 4
SIDE = 8
LANES = 256
SLOT = 24
BLOCK = 4
F32 = jnp.float32
BF16 = jnp.bfloat16


def vmem_specs(count):
    return [pl.BlockSpec(memory_space=pltpu.VMEM) for _ in range(count)]


def smem_spec():
    return pl.BlockSpec(memory_space=pltpu.SMEM)


def params(mebibytes):
    return pltpu.CompilerParams(vmem_limit_bytes=mebibytes << 20)


def near_core(*arrays):
    return [pltpu.with_memory_space_constraint(array, pltpu.VMEM) for array in arrays]


def in_hbm(*arrays):
    return [pltpu.with_memory_space_constraint(array, pltpu.HBM) for array in arrays]


def far_specs(count):
    return [pl.BlockSpec(memory_space=pl.ANY) for _ in range(count)]


def copies(pairs, sems):
    return [pltpu.make_async_copy(src, dst, sems.at[i]) for i, (src, dst) in enumerate(pairs)]


BANDS = 22
EDGE = 4


def pack_kernel(holder_ref, tile_ref, values_ref, out_ref, wide_ref, *, shift):
    count, width = values_ref.shape[1], values_ref.shape[2]
    slots = out_ref.shape[0] // SLOT
    named = jnp.broadcast_to(holder_ref[...].astype(F32), (count, count))
    first = lax.broadcasted_iota(jnp.int32, (count, count), 0)
    second = lax.broadcasted_iota(jnp.int32, (count, count), 1)
    same = (jnp.transpose(named) == named) & (first < second)
    ranks = jnp.sum(same.astype(F32), axis=0, keepdims=True)
    chosen = holder_ref[...] * CAPACITY + ranks.astype(jnp.int32)
    onehot = lax.broadcasted_iota(jnp.int32, (slots, count), 0) == chosen
    onehot = onehot.astype(F32).astype(BF16)
    numbers = jnp.broadcast_to((tile_ref[...] + 1).astype(F32), (width, count))
    numbers = jnp.transpose(numbers).astype(BF16)
    cell = lax.broadcasted_iota(jnp.int32, (width, 2 * width), 0)
    lane = lax.broadcasted_iota(jnp.int32, (width, 2 * width), 1)
    high = lane - (cell - (width - EDGE)) * SLOT
    low = lane - width - cell * SLOT
    channel = jnp.where(
        lane < width, jnp.where(cell >= width - EDGE, high, -1), jnp.where(cell < EDGE, low, -1)
    )
    edges = None
    for k in range(BANDS + 1):
        values = values_ref[k] if k < BANDS else numbers
        if k < BANDS:
            wide_ref[pl.ds(k, slots, stride=SLOT), :] = jnp.dot(
                onehot, values, preferred_element_type=F32
            )
        spread = (channel == k).astype(F32).astype(BF16)
        part = jnp.dot(values, spread, preferred_element_type=F32)
        edges = part if edges is None else edges + part
    placed = jnp.dot(onehot, edges.astype(BF16), preferred_element_type=F32)
    own = jnp.dot(onehot, numbers, preferred_element_type=F32)
    before = pltpu.roll(placed[:, 0:width], shift, 0)
    after = pltpu.roll(placed[:, width : 2 * width], slots - shift, 0)
    at = lax.broadcasted_iota(jnp.int32, (slots, width), 1)
    wide_ref[pl.ds(BANDS, slots, stride=SLOT), :] = jnp.where(at == BANDS + 1, own, before)
    wide_ref[pl.ds(BANDS + 1, slots, stride=SLOT), :] = after
    out_ref[...] = wide_ref[...].astype(BF16)


def pack_blocks(holders, tiles, values, slot_count, shift):
    width = values.shape[2]
    return pl.pallas_call(
        functools.partial(pack_kernel, shift=shift),
        out_shape=jax.ShapeDtypeStruct((slot_count * SLOT, width), BF16),
        in_specs=vmem_specs(3),
        out_specs=vmem_specs(1)[0],
        scratch_shapes=[pltpu.VMEM((slot_count * SLOT, width), F32)],
        compiler_params=params(12),
        name="pack_blocks",
    )(holders.reshape(1, -1), tiles.reshape(1, -1), jnp.transpose(values, (1, 0, 2)))


def put_shifted(dst_ref, row, width, act):
    size, channels = act.shape
    at = pl.ds(row * width, size)
    dst_ref[at, LANES : LANES + channels] = act.astype(BF16)
    dst_ref[at, 0:channels] = pltpu.roll(act, 1, 0).astype(BF16)
    dst_ref[at, 2 * LANES : 2 * LANES + channels] = pltpu.roll(act, size - 1, 0).astype(BF16)


def conv_block(src_ref, row, rows, width, w_ref, side, flip):
    acc = None
    taken = w_ref.shape[1 + side]
    for p in range(3):
        at = pl.ds((row + p) * width, rows * width)
        for q in range(3):
            tap = 3 * p + q
            part = lax.dot_general(
                src_ref[at, q * LANES : q * LANES + taken],
                w_ref[8 - tap if flip else tap],
                (((1,), (side,)), ((), ())),
                preferred_element_type=F32,
            )
            acc = part if acc is None else acc + part
    return acc


def conv_layer(rows, compute, finish, acc_a, acc_b):
    full, rest = divmod(rows, BLOCK)
    first = compute(0, BLOCK)
    size, channels = first.shape
    unit = size // BLOCK

    def keep(acc, value):
        acc[0 : value.shape[0], 0:channels] = value

    def kept(acc, n):
        return acc[0 : n * unit, 0:channels]

    keep(acc_a, first)
    pairs = (full - 1) // 2

    def body(j, carry):
        row = 2 * BLOCK * j
        keep(acc_b, compute(row + BLOCK, BLOCK))
        finish(row, BLOCK, kept(acc_a, BLOCK))
        keep(acc_a, compute(row + 2 * BLOCK, BLOCK))
        finish(row + BLOCK, BLOCK, kept(acc_b, BLOCK))
        return carry

    lax.fori_loop(0, pairs, body, 0)
    done = 2 * pairs
    last, free = acc_a, acc_b
    if full - 1 > done:
        keep(acc_b, compute((done + 1) * BLOCK, BLOCK))
        finish(done * BLOCK, BLOCK, kept(acc_a, BLOCK))
        last, free = acc_b, acc_a
    if rest:
        keep(free, compute(full * BLOCK, rest))
    finish((full - 1) * BLOCK, BLOCK, kept(last, BLOCK))
    if rest:
        finish(full * BLOCK, rest, kept(free, rest))


def either(flag, yes, no):
    return jnp.where(flag == 1, yes, no)


def turn_kernel(place_ref, state_ref, own_ref, near_ref, far_ref, low_ref, high_ref):
    _, rows, cells = state_ref.shape
    for r in range(rows):
        part = jnp.transpose(state_ref[:, r, :])
        own_ref[r * cells : (r + 1) * cells, :] = part.astype(BF16)
        low_ref[r * SIDE : (r + 1) * SIDE, :] = part[0:SIDE, :]
        high_ref[r * SIDE : (r + 1) * SIDE, :] = part[cells - SIDE : cells, :]
    low = low_ref[...]
    high = high_ref[...]
    near_ref[...] = either(place_ref[0], high, low).astype(BF16)
    far_ref[...] = either(place_ref[0], low, high).astype(BF16)


def turn_state(place, state):
    channels, rows, cells = state.shape
    edge = (rows * SIDE, channels)
    return pl.pallas_call(
        turn_kernel,
        out_shape=(
            pltpu.HBM((rows * cells, channels), BF16),
            jax.ShapeDtypeStruct(edge, BF16),
            jax.ShapeDtypeStruct(edge, BF16),
        ),
        in_specs=[smem_spec()] + vmem_specs(1),
        out_specs=tuple(vmem_specs(3)),
        scratch_shapes=[pltpu.VMEM(edge, F32)] * 2,
        compiler_params=params(8),
        name="turn_state",
    )(place, *near_core(state))


def framed_row(place_ref, own_ref, near_ref, far_ref, r, cells):
    at = pl.ds(r * SIDE, SIDE)
    near = near_ref[at, :].astype(F32)
    far = far_ref[at, :].astype(F32)
    own = own_ref[pl.ds(r * cells, cells), :].astype(F32)
    left = either(place_ref[0], far, near)
    right = either(place_ref[0], near, far)
    return jnp.concatenate([left, own, right], axis=0)


def frame_kernel(place_ref, own_ref, lon_near_ref, lon_far_ref, near_ref, far_ref):
    rows = lon_near_ref.shape[0] // SIDE
    cells = own_ref.shape[0] // rows
    width = cells + 2 * SIDE
    for i in range(HALO):
        top = framed_row(place_ref, own_ref, lon_near_ref, lon_far_ref, i, cells)
        low = framed_row(place_ref, own_ref, lon_near_ref, lon_far_ref, rows - HALO + i, cells)
        at = pl.ds(i * width, width)
        near_ref[at, :] = either(place_ref[1], low, top).astype(BF16)
        far_ref[at, :] = either(place_ref[1], top, low).astype(BF16)


def frame_rows(place, own, lon_near, lon_far, width):
    shape = (HALO * width, own.shape[1])
    return pl.pallas_call(
        frame_kernel,
        out_shape=(jax.ShapeDtypeStruct(shape, BF16),) * 2,
        in_specs=[smem_spec()] + vmem_specs(3),
        out_specs=tuple(vmem_specs(2)),
        compiler_params=params(8),
        name="frame_rows",
    )(place, *in_hbm(own), lon_near, lon_far)


def weight_scratch(weights):
    return [pltpu.VMEM(weight.shape, BF16) for weight in weights]


def forward_kernel(
    place_ref, own_ref, lon_near_ref, lon_far_ref, lat_near_ref, lat_far_ref, op_ref, w0_far, wm_far, w3_far,
    pre_far, pred_ref, edge_ref, d0_far, d1_far, d2_far,
    buf_a, buf_b, acc_a, acc_b, w0, wm, w3, pre_ref, clean_a, clean_b, d0, d1, d2, in_sems, out_sems,
):
    rows, width, channels = pre_ref.shape
    cells = width - 2 * SIDE
    weights = (w0, wm.at[0], wm.at[1], w3)
    slopes = (d0, d1, d2)
    loads = copies(
        ((w0_far, w0), (wm_far.at[0], wm.at[0]), (wm_far.at[1], wm.at[1]), (w3_far, w3)), in_sems
    )
    stores = copies(((d0, d0_far), (d1, d1_far), (d2, d2_far), (pre_ref, pre_far)), out_sems)
    for load in loads:
        load.start()

    def fill(i, carry):
        put_shifted(buf_a, i + HALO, width, framed_row(place_ref, own_ref, lon_near_ref, lon_far_ref, i, cells))
        return carry

    lax.fori_loop(0, rows, fill, 0)
    for i in range(HALO):
        at = pl.ds(i * width, width)
        near = lat_near_ref[at, :].astype(F32)
        far = lat_far_ref[at, :].astype(F32)
        put_shifted(buf_a, i, width, either(place_ref[1], far, near))
        put_shifted(buf_a, i + HALO + rows, width, either(place_ref[1], near, far))
    src, dst = buf_a, buf_b
    for layer in range(LAYERS):
        margin = HALO - 1 - layer
        count = rows + 2 * margin

        def compute(row, n, src=src, layer=layer):
            return conv_block(src, row, n, width, weights[layer], 0 if layer == 0 else 1, False)

        loads[layer].wait()

        if layer < LAYERS - 1:

            def finish(row, n, value, dst=dst, layer=layer):
                gate = 0.5 + 0.5 * jnp.tanh(0.5 * value)
                act = value * gate
                slope = gate + act * (1.0 - gate)
                slopes[layer][pl.ds(row * width, n * width), :] = slope.astype(BF16)
                put_shifted(dst, row, width, act)

        else:

            def finish(row, n, value):
                for i in range(n):
                    part = value[i * width : (i + 1) * width, :]
                    pre_ref[row + i] = part
                    own = framed_row(place_ref, own_ref, lon_near_ref, lon_far_ref, row + i, cells)
                    clean = (own + part).astype(BF16)
                    at = pl.ds((row + i) * width, width)
                    clean_a[at, :] = clean[:, 0:128].astype(F32)
                    clean_b[at, 0 : channels - 128] = clean[:, 128:channels].astype(F32)
                    pred_ref[row + i] = lax.dot_general(
                        op_ref[:, 0:channels],
                        clean[SIDE : SIDE + cells, :],
                        (((1,), (1,)), ((), ())),
                        preferred_element_type=F32,
                    )

        conv_layer(count, compute, finish, acc_a, acc_b)
        if layer < LAYERS - 1:
            size = margin * width

            def clear(first, dst=dst, layer=layer, size=size):
                slopes[layer][first : first + size, :] = jnp.zeros((size, LANES), BF16)
                dst[first : first + size, :] = jnp.zeros((size, 3 * LANES), BF16)

            @pl.when(place_ref[2] == 1)
            def _():
                clear(0)

            @pl.when(place_ref[3] == 1)
            def _(count=count, size=size):
                clear(count * width - size)

        stores[layer].start()
        src, dst = dst, src
    tall = jnp.concatenate([op_ref[:, 0:channels].astype(F32), jnp.zeros((96, channels), F32)], axis=0).astype(BF16)
    for end, first in ((0, SIDE - EDGE), (1, SIDE + cells)):
        total = None
        for c in range(EDGE):
            at = pl.ds(first + c, rows, stride=width)
            clean = jnp.concatenate([clean_a[at, :], clean_b[at, :]], axis=1)[:, 0:channels]
            part = lax.dot_general(
                clean.astype(BF16), tall, (((1,), (1,)), ((), ())), preferred_element_type=F32
            )
            part = pltpu.roll(part, c * SLOT, 1) if c else part
            total = part if total is None else total + part
        edge_ref[end] = total
    for store in stores:
        store.wait()


def forward_pass(place, own, lon, lat, weights, operator, rows, width):
    slopes = [((rows + 2 * (HALO - 1 - layer)) * width, LANES) for layer in range(LAYERS - 1)]
    pre = (rows, width, own.shape[1])
    padded = (rows + 2 * HALO) * width
    return pl.pallas_call(
        forward_kernel,
        out_shape=(
            pltpu.HBM(pre, F32),
            pltpu.HBM((rows, operator.shape[0], width - 2 * SIDE), F32),
            pltpu.HBM((2, rows, 128), F32),
        )
        + tuple(pltpu.HBM(shape, BF16) for shape in slopes),
        in_specs=[smem_spec()] + vmem_specs(6) + far_specs(3),
        out_specs=tuple(far_specs(1) + vmem_specs(2) + far_specs(3)),
        scratch_shapes=[pltpu.VMEM((padded, 3 * LANES), BF16)] * 2
        + [pltpu.VMEM((BLOCK * width, LANES), F32)] * 2
        + weight_scratch(weights)
        + [pltpu.VMEM(pre, F32)] + [pltpu.VMEM((rows * width, 128), F32)] * 2
        + [pltpu.VMEM(shape, BF16) for shape in slopes]
        + [pltpu.SemaphoreType.DMA((LAYERS,)), pltpu.SemaphoreType.DMA((LAYERS,))],
        compiler_params=params(34),
        name="forward_pass",
    )(place, *in_hbm(own), *lon, *lat, operator, *in_hbm(*weights))


LEAD = HALO + 1


def slope_rows(layer, first):
    return first - (layer - HALO + 1)


def edge_kernel(
    place_ref, recv_ref, pred_ref, pred_edge_ref, op_ref, prec_ref, prec_edge_ref,
    d0_far, d1_far, d2_far, w0_far, wm_far, w3_far,
    pulled_ref, near_ref, far_ref, s0_ref, s1_ref, s2_ref,
    wide_ref, sums_ref, field_a, field_b, buf_a, buf_b, acc_a, acc_b, w0, wm, w3, d_ref, in_sems,
):
    rows, cells, channels = pred_ref.shape[0], pred_ref.shape[2], near_ref.shape[1]
    width = cells + 2 * SIDE
    slots = recv_ref.shape[0] // SLOT
    weights = (w0, wm.at[0], wm.at[1], w3)
    strips = (s0_ref, s1_ref, s2_ref)
    size = HALO * width
    pairs = [(w3_far, w3), (wm_far.at[1], wm.at[1]), (wm_far.at[0], wm.at[0]), (w0_far, w0)]
    for layer, source in ((2, d2_far), (1, d1_far), (0, d0_far)):
        for end in range(2):
            first = layer + 1 - HALO if end == 0 else rows - 1 - layer
            at = slope_rows(layer, first) * width
            pairs.append((source.at[pl.ds(at, size)], d_ref.at[layer, end]))
    loads = copies(pairs, in_sems)
    for load in loads:
        load.start()

    nothing = jnp.zeros((4 * width, 3 * LANES), BF16)
    buf_a[width : 5 * width, :] = nothing
    buf_a[(rows + 5) * width : (rows + 9) * width, :] = nothing
    buf_b[0 : 4 * width, :] = nothing
    buf_b[(rows + 6) * width : (rows + 10) * width, :] = nothing

    wide_ref[...] = recv_ref[...].astype(F32)
    sums_ref[...] = jnp.zeros(sums_ref.shape, F32)
    sides = [wide_ref[pl.ds(BANDS + end, slots, stride=SLOT), :] for end in range(2)]
    lane = lax.broadcasted_iota(jnp.int32, (slots, cells), 1).astype(F32)
    own = sides[0][:, BANDS + 1 : BANDS + 2]
    before = sides[0][:, BANDS : BANDS + 1] + rows
    after = sides[1][:, BANDS : BANDS + 1] + 2 * rows
    wanted = jnp.where(lane < rows, own, jnp.where(lane < 2 * rows, before, after))
    least = jnp.where(lane < rows, 0.0, jnp.where(lane < 2 * rows, 1.0 * rows, 2.0 * rows))
    match = (wanted == lane + 1.0) & (wanted > least) & (lane < 3 * rows)
    onehot = jnp.transpose(match.astype(F32))[0 : 3 * rows, :].astype(BF16)
    held = jnp.dot(onehot, jnp.ones((slots, cells), BF16), preferred_element_type=F32)
    own_hot = onehot[0:rows, :]
    for k in range(BANDS):
        part = wide_ref[pl.ds(k, slots, stride=SLOT), :].astype(BF16)
        sums_ref[pl.ds(k, rows, stride=32), :] = jnp.dot(own_hot, part, preferred_element_type=F32)
    nothing = jnp.zeros((SIDE, 128), F32)
    for r in range(rows):
        summed = sums_ref[r * 32 : (r + 1) * 32, :]
        weighted = (summed - held[r : r + 1, :] * pred_ref[r]) * prec_ref[...]
        at = r * width
        value = jnp.dot(
            jnp.transpose(weighted).astype(BF16), op_ref[...], preferred_element_type=F32
        )
        for field, part in ((field_a, value[:, 0:128]), (field_b, value[:, 128:LANES])):
            field[at : at + SIDE, :] = nothing
            field[at + SIDE : at + SIDE + cells, :] = part
            field[at + SIDE + cells : at + width, :] = nothing
    short = op_ref[...].astype(F32)[0:SLOT, :]
    for end, first in ((0, SIDE - EDGE), (1, SIDE + cells)):
        part = onehot[(1 + end) * rows : (2 + end) * rows, :]
        summed = jnp.dot(part, sides[end].astype(BF16), preferred_element_type=F32)
        count = held[(1 + end) * rows : (2 + end) * rows, :]
        weighted = ((summed - count * pred_edge_ref[end]) * prec_edge_ref[...]).astype(BF16)
        for c in range(EDGE):
            above = [jnp.zeros((c * SLOT, LANES), F32)] if c else []
            below = jnp.zeros((128 - (c + 1) * SLOT, LANES), F32)
            picked = jnp.concatenate(above + [short, below], axis=0).astype(BF16)
            value = jnp.dot(weighted, picked, preferred_element_type=F32)
            at = pl.ds(first + c, rows, stride=width)
            field_a[at, :] = value[:, 0:128]
            field_b[at, :] = value[:, 128:LANES]
    for r in range(rows):
        at = slice(r * width, (r + 1) * width)
        row = jnp.concatenate([field_a[at, :], field_b[at, :]], axis=1)[:, 0:channels]
        pulled_ref[r] = row
        if r < HALO or r >= rows - HALO:
            put_shifted(buf_a, r + LEAD, width, row)

    src, dst = buf_a, buf_b
    for layer in range(LAYERS - 1, -1, -1):
        margin = LAYERS - layer
        tops = (-margin, rows + margin - HALO)
        accs = (acc_a, acc_b)
        loads[LAYERS - 1 - layer].wait()
        for end in range(2):
            value = conv_block(
                src, tops[end] + LEAD - 1, HALO, width, weights[layer], 1 if layer == 0 else 0, True
            )
            accs[end][:, 0 : value.shape[1]] = value
        if layer > 0:
            for end in range(2):
                loads[LAYERS + 2 * (LAYERS - 1 - layer) + end].wait()
                value = accs[end][...] * d_ref[layer - 1, end].astype(F32)
                put_shifted(dst, tops[end] + LEAD, width, value)
                half = size // 2
                kept = value[half:, :] if end == 0 else value[0:half, :]
                strips[layer - 1][end * half : (end + 1) * half, :] = kept.astype(BF16)
        else:
            for i in range(HALO):
                at = slice(i * width + SIDE, i * width + SIDE + cells)
                top = acc_a[at, 0:channels]
                low = acc_b[at, 0:channels]
                out = slice(i * cells, (i + 1) * cells)
                near_ref[out, :] = either(place_ref[1], low, top).astype(BF16)
                far_ref[out, :] = either(place_ref[1], top, low).astype(BF16)
        src, dst = dst, src


def edge_pass(place, recv, pred, pred_edge, slopes, operator, precision, precision_edge, weights, channels):
    rows, cells = pred.shape[0], pred.shape[2]
    width = cells + 2 * SIDE
    padded = (rows + 2 * LEAD) * width
    size = HALO * width
    return pl.pallas_call(
        edge_kernel,
        out_shape=(
            pltpu.HBM((rows, width, channels), F32),
            jax.ShapeDtypeStruct((HALO * cells, channels), BF16),
            jax.ShapeDtypeStruct((HALO * cells, channels), BF16),
        )
        + tuple(pltpu.HBM((size, LANES), BF16) for _ in range(LAYERS - 1)),
        in_specs=[smem_spec()] + vmem_specs(6) + far_specs(6),
        out_specs=tuple(vmem_specs(6)),
        scratch_shapes=[
            pltpu.VMEM(recv.shape, F32),
            pltpu.VMEM((rows * 32, recv.shape[1]), F32),
            pltpu.VMEM((rows * width, 128), F32),
            pltpu.VMEM((rows * width, 128), F32),
        ]
        + [pltpu.VMEM((padded, 3 * LANES), BF16)] * 2
        + [pltpu.VMEM((size, LANES), F32)] * 2
        + weight_scratch(weights)
        + [pltpu.VMEM((LAYERS - 1, 2, size, LANES), BF16), pltpu.SemaphoreType.DMA((LAYERS + 6,))],
        compiler_params=params(34),
        name="edge_pass",
    )(place, recv, *in_hbm(pred, pred_edge), operator, precision, precision_edge, *in_hbm(*slopes, *weights))


def inner_kernel(
    level_ref, pulled_ref, s0_ref, s1_ref, s2_ref, pre_far, d0_far, d1_far, d2_far, w0_far, wm_far, w3_far,
    own_ref,
    buf_a, buf_b, acc_a, acc_b, w0, wm, w3, pre_ref, d0, d1, d2, in_sems,
):
    rows, width, _ = pulled_ref.shape
    cells = width - 2 * SIDE
    inverse = 1.0 / (level_ref[...] * level_ref[...])
    weights = (w0, wm.at[0], wm.at[1], w3)
    strips = (s0_ref, s1_ref, s2_ref)
    slopes = (d0, d1, d2)
    pairs = [(w3_far, w3)]
    for layer, source, weight in ((2, d2_far, 1), (1, d1_far, 0), (0, d0_far, None)):
        first = layer + 1
        count = slopes[layer].shape[0]
        pairs.append((source.at[pl.ds(slope_rows(layer, first) * width, count)], slopes[layer]))
        pairs.append((w0_far, w0) if weight is None else (wm_far.at[weight], wm.at[weight]))
    pairs.append((pre_far, pre_ref))
    loads = copies(pairs, in_sems)
    for load in loads:
        load.start()

    def fill(r, carry):
        put_shifted(buf_a, r + LEAD, width, pulled_ref[r])
        return carry

    lax.fori_loop(0, rows, fill, 0)
    loads[0].wait()
    src, dst = buf_a, buf_b
    half = HALO // 2 * width
    for layer in range(LAYERS - 1, -1, -1):
        begin = layer
        count = rows - 2 * layer

        def compute(row, n, src=src, layer=layer, begin=begin):
            return conv_block(
                src, row + begin + LEAD - 1, n, width, weights[layer], 1 if layer == 0 else 0, True
            )

        if layer > 0:
            kept = strips[layer - 1]
            put_shifted(dst, layer - 2 + LEAD, width, kept[0:half, :].astype(F32))
            put_shifted(dst, rows - layer + LEAD, width, kept[half:, :].astype(F32))
            loads[2 * (LAYERS - 1 - layer) + 1].wait()

            def finish(row, n, value, dst=dst, layer=layer, begin=begin):
                slope = slopes[layer - 1][pl.ds(row * width, n * width), :]
                put_shifted(dst, row + begin + LEAD, width, value * slope.astype(F32))

            conv_layer(count, compute, finish, acc_a, acc_b)
            loads[2 * (LAYERS - 1 - layer) + 2].wait()
        else:
            loads[-1].wait()

            def finish(row, n, value):
                for i in range(n):
                    total = pre_ref[row + i] * inverse + pulled_ref[row + i] + value[i * width : (i + 1) * width, :]
                    own_ref[row + i] = total[SIDE : SIDE + cells, :]

            conv_layer(count, compute, finish, acc_a, acc_b)
        src, dst = dst, src


def inner_pass(level, pulled, strips, pre, slopes, weights):
    rows, width, channels = pre.shape
    padded = (rows + 2 * LEAD) * width
    kept = [((rows - 2 * (layer + 1)) * width, LANES) for layer in range(LAYERS - 1)]
    return pl.pallas_call(
        inner_kernel,
        out_shape=pltpu.HBM((rows, width - 2 * SIDE, channels), F32),
        in_specs=vmem_specs(5) + far_specs(7),
        out_specs=vmem_specs(1)[0],
        scratch_shapes=[pltpu.VMEM((padded, 3 * LANES), BF16)] * 2
        + [pltpu.VMEM((BLOCK * width, LANES), F32)] * 2
        + weight_scratch(weights)
        + [pltpu.VMEM(pre.shape, F32)]
        + [pltpu.VMEM(shape, BF16) for shape in kept]
        + [pltpu.SemaphoreType.DMA((2 * LAYERS,))],
        compiler_params=params(34),
        name="inner_pass",
    )(level, *in_hbm(pulled, *strips, pre, *slopes, *weights))


def final_kernel(place_ref, step_ref, own_ref, near_ref, far_ref, state_ref, noise_ref, out_ref):
    rows, cells = own_ref.shape[0], own_ref.shape[1]
    step = step_ref[...]
    spread = jnp.sqrt(2.0 * step)
    for r in range(rows):
        total = own_ref[r]
        at = r if r < HALO else r - (rows - HALO)
        if r < HALO or r >= rows - HALO:
            near = near_ref[at * cells : (at + 1) * cells, :].astype(F32)
            far = far_ref[at * cells : (at + 1) * cells, :].astype(F32)
            if r < HALO:
                total = total + either(place_ref[1], far, near)
            else:
                total = total + either(place_ref[1], near, far)
        out_ref[:, r, :] = state_ref[:, r, :] + step * jnp.transpose(total) + spread * noise_ref[:, r, :]


def final_pass(place, step, own, near, far, state, noise):
    return pl.pallas_call(
        final_kernel,
        out_shape=jax.ShapeDtypeStruct(state.shape, F32),
        in_specs=[smem_spec()] + vmem_specs(6),
        out_specs=vmem_specs(1)[0],
        compiler_params=params(16),
        name="final_pass",
    )(place, step, *in_hbm(own), near, far, *near_core(state, noise))


def swap_pairs(size, first, wrap):
    pairs = []
    for low in range(first, size if wrap else size - 1, 2):
        high = (low + 1) % size
        pairs += [(low, high), (high, low)]
    return pairs


def swap(axis, wrap, near, far):
    size = lax.axis_size(axis)
    return lax.ppermute(near, axis, swap_pairs(size, 0, wrap)), lax.ppermute(far, axis, swap_pairs(size, 1, wrap))


def pad_to(values, shape):
    return jnp.pad(values, [(0, n - m) for m, n in zip(values.shape, shape)])


def shards(
    state,
    noise,
    first_kernel,
    middle_kernels,
    last_kernel,
    obs_values,
    obs_holder,
    obs_tile,
    obs_operator,
    obs_precision,
    noise_level,
    step_size,
):
    channels, rows, cells = state.shape
    width = cells + 2 * SIDE
    weights = (jnp.transpose(first_kernel, (0, 2, 1)), middle_kernels, last_kernel)
    lon, lat = lax.axis_index("lon"), lax.axis_index("lat")
    bands = lax.axis_size("lat")
    place = jnp.stack([lon % 2 == 0, lat % 2 == 0, lat == 0, lat == bands - 1]).astype(jnp.int32)

    holders = lax.axis_size(("lon", "lat"))
    packed = pack_blocks(obs_holder, obs_tile, obs_values, holders * CAPACITY, bands * CAPACITY)
    own, *edges = turn_state(place, state)
    lon_halo = swap("lon", True, *edges)
    framed = frame_rows(place, own, *lon_halo, width)
    packed, framed = lax.optimization_barrier((packed, framed))
    lat_halo = swap("lat", False, *framed)
    recv = lax.all_to_all(
        packed.reshape(holders, CAPACITY * SLOT, cells), ("lon", "lat"), split_axis=0, concat_axis=0, tiled=True
    ).reshape(packed.shape)

    operator = pad_to(obs_operator, (32, LANES))
    precision = pad_to(obs_precision[:, None], (32, 1))
    precision_edge = pad_to(jnp.tile(pad_to(obs_precision, (SLOT,)), EDGE)[None, :], (1, 128))
    pre, pred, pred_edge, *slopes = forward_pass(place, own, lon_halo, lat_halo, weights, operator, rows, width)
    pulled, near, far, *strips = edge_pass(
        place, recv, pred, pred_edge, slopes, operator, precision, precision_edge, weights, channels
    )
    near, far = swap("lat", False, near, far)
    own = inner_pass(noise_level.reshape(1, 1), pulled, strips, pre, slopes, weights)
    return final_pass(place, step_size.reshape(1, 1), own, near, far, state, noise)


def solution(mesh):
    placed = (
        P(None, "lat", "lon"),
        P(None, "lat", "lon"),
        P(),
        P(),
        P(),
        P(("lon", "lat"), None, None),
        P(("lon", "lat"), None),
        P(("lon", "lat")),
        P(),
        P(),
        P(),
        P(),
    )

    return jax.shard_map(
        shards, mesh=mesh, in_specs=placed, out_specs=P(None, "lat", "lon"), check_vma=False
    )
```

```python
import functools

import jax
import jax.numpy as jnp
from jax import lax
from jax.experimental import pallas as pl
from jax.experimental.pallas import tpu as pltpu
from jax.sharding import PartitionSpec as P


LAYERS = 4
CAPACITY = 2
HALO = 4
SIDE = 8
LANES = 256
SLOT = 24
BLOCK = 4
F32 = jnp.float32
BF16 = jnp.bfloat16


def vmem_specs(count):
    return [pl.BlockSpec(memory_space=pltpu.VMEM) for _ in range(count)]


def smem_spec():
    return pl.BlockSpec(memory_space=pltpu.SMEM)


def params(mebibytes):
    return pltpu.CompilerParams(vmem_limit_bytes=mebibytes << 20)


def in_hbm(*arrays):
    return [pltpu.with_memory_space_constraint(array, pltpu.HBM) for array in arrays]


def far_specs(count):
    return [pl.BlockSpec(memory_space=pl.ANY) for _ in range(count)]


def copies(pairs, sems):
    return [pltpu.make_async_copy(src, dst, sems.at[i]) for i, (src, dst) in enumerate(pairs)]


BANDS = 22
EDGE = 4


def pack_kernel(holder_ref, tile_ref, values_ref, out_ref, wide_ref, *, shift):
    count, width = values_ref.shape[1], values_ref.shape[2]
    slots = out_ref.shape[0] // SLOT
    named = jnp.broadcast_to(holder_ref[...].astype(F32), (count, count))
    first = lax.broadcasted_iota(jnp.int32, (count, count), 0)
    second = lax.broadcasted_iota(jnp.int32, (count, count), 1)
    same = (jnp.transpose(named) == named) & (first < second)
    ranks = jnp.sum(same.astype(F32), axis=0, keepdims=True)
    chosen = holder_ref[...] * CAPACITY + ranks.astype(jnp.int32)
    onehot = lax.broadcasted_iota(jnp.int32, (slots, count), 0) == chosen
    onehot = onehot.astype(F32).astype(BF16)
    numbers = jnp.broadcast_to((tile_ref[...] + 1).astype(F32), (width, count))
    numbers = jnp.transpose(numbers).astype(BF16)
    cell = lax.broadcasted_iota(jnp.int32, (width, 2 * width), 0)
    lane = lax.broadcasted_iota(jnp.int32, (width, 2 * width), 1)
    high = lane - (cell - (width - EDGE)) * SLOT
    low = lane - width - cell * SLOT
    channel = jnp.where(
        lane < width, jnp.where(cell >= width - EDGE, high, -1), jnp.where(cell < EDGE, low, -1)
    )
    edges = None
    for k in range(BANDS + 1):
        values = values_ref[k] if k < BANDS else numbers
        if k < BANDS:
            wide_ref[pl.ds(k, slots, stride=SLOT), :] = jnp.dot(
                onehot, values, preferred_element_type=F32
            )
        spread = (channel == k).astype(F32).astype(BF16)
        part = jnp.dot(values, spread, preferred_element_type=F32)
        edges = part if edges is None else edges + part
    placed = jnp.dot(onehot, edges.astype(BF16), preferred_element_type=F32)
    own = jnp.dot(onehot, numbers, preferred_element_type=F32)
    before = pltpu.roll(placed[:, 0:width], shift, 0)
    after = pltpu.roll(placed[:, width : 2 * width], slots - shift, 0)
    at = lax.broadcasted_iota(jnp.int32, (slots, width), 1)
    wide_ref[pl.ds(BANDS, slots, stride=SLOT), :] = jnp.where(at == BANDS + 1, own, before)
    wide_ref[pl.ds(BANDS + 1, slots, stride=SLOT), :] = after
    out_ref[...] = wide_ref[...].astype(BF16)


def pack_blocks(holders, tiles, values, slot_count, shift):
    width = values.shape[2]
    return pl.pallas_call(
        functools.partial(pack_kernel, shift=shift),
        out_shape=jax.ShapeDtypeStruct((slot_count * SLOT, width), BF16),
        in_specs=vmem_specs(3),
        out_specs=vmem_specs(1)[0],
        scratch_shapes=[pltpu.VMEM((slot_count * SLOT, width), F32)],
        compiler_params=params(12),
        name="pack_blocks",
    )(*in_hbm(holders.reshape(1, -1), tiles.reshape(1, -1), jnp.transpose(values, (1, 0, 2))))


def put_shifted(dst_ref, row, width, act):
    size, channels = act.shape
    at = pl.ds(row * width, size)
    dst_ref[at, LANES : LANES + channels] = act.astype(BF16)
    dst_ref[at, 0:channels] = pltpu.roll(act, 1, 0).astype(BF16)
    dst_ref[at, 2 * LANES : 2 * LANES + channels] = pltpu.roll(act, size - 1, 0).astype(BF16)


def conv_block(src_ref, row, rows, width, w_ref, side, flip):
    acc = None
    taken = w_ref.shape[1 + side]
    for p in range(3):
        at = pl.ds((row + p) * width, rows * width)
        for q in range(3):
            tap = 3 * p + q
            part = lax.dot_general(
                src_ref[at, q * LANES : q * LANES + taken],
                w_ref[8 - tap if flip else tap],
                (((1,), (side,)), ((), ())),
                preferred_element_type=F32,
            )
            acc = part if acc is None else acc + part
    return acc


def conv_layer(rows, compute, finish, acc_a, acc_b):
    full, rest = divmod(rows, BLOCK)
    first = compute(0, BLOCK)
    size, channels = first.shape
    unit = size // BLOCK

    def keep(acc, value):
        acc[0 : value.shape[0], 0:channels] = value

    def kept(acc, n):
        return acc[0 : n * unit, 0:channels]

    keep(acc_a, first)
    pairs = (full - 1) // 2

    def body(j, carry):
        row = 2 * BLOCK * j
        keep(acc_b, compute(row + BLOCK, BLOCK))
        finish(row, BLOCK, kept(acc_a, BLOCK))
        keep(acc_a, compute(row + 2 * BLOCK, BLOCK))
        finish(row + BLOCK, BLOCK, kept(acc_b, BLOCK))
        return carry

    if pairs > 1:
        lax.fori_loop(0, pairs, body, 0)
    elif pairs:
        body(0, 0)
    done = 2 * pairs
    last, free = acc_a, acc_b
    if full - 1 > done:
        keep(acc_b, compute((done + 1) * BLOCK, BLOCK))
        finish(done * BLOCK, BLOCK, kept(acc_a, BLOCK))
        last, free = acc_b, acc_a
    if rest:
        keep(free, compute(full * BLOCK, rest))
    finish((full - 1) * BLOCK, BLOCK, kept(last, BLOCK))
    if rest:
        finish(full * BLOCK, rest, kept(free, rest))


def either(flag, yes, no):
    return jnp.where(flag == 1, yes, no)


def turn_kernel(
    place_ref, state_far, own_ref, outer_ref, near_ref, far_ref, state_ref, low_ref, high_ref, sems
):
    _, rows, cells = state_ref.shape
    half = rows // 2
    parts = [pl.ds(0, half), pl.ds(half, half)]
    loads = copies([(state_far.at[:, at, :], state_ref.at[:, at, :]) for at in parts], sems)
    for load in loads:
        load.start()
    for r in range(rows):
        if r % half == 0:
            loads[r // half].wait()
        part = jnp.transpose(state_ref[:, r, :])
        turned = part.astype(BF16)
        own_ref[r * cells : (r + 1) * cells, :] = turned
        if r < HALO or r >= rows - HALO:
            at = outer_row(r, rows) * cells
            outer_ref[at : at + cells, :] = turned
        low_ref[r * SIDE : (r + 1) * SIDE, :] = part[0:SIDE, :]
        high_ref[r * SIDE : (r + 1) * SIDE, :] = part[cells - SIDE : cells, :]
    low = low_ref[...]
    high = high_ref[...]
    near_ref[...] = either(place_ref[0], high, low).astype(BF16)
    far_ref[...] = either(place_ref[0], low, high).astype(BF16)


def outer_row(r, rows):
    return r if r < HALO else r - (rows - HALO) + HALO


def turn_state(place, state):
    channels, rows, cells = state.shape
    edge = (rows * SIDE, channels)
    return pl.pallas_call(
        turn_kernel,
        out_shape=(
            pltpu.HBM((rows * cells, channels), BF16),
            jax.ShapeDtypeStruct((2 * HALO * cells, channels), BF16),
            jax.ShapeDtypeStruct(edge, BF16),
            jax.ShapeDtypeStruct(edge, BF16),
        ),
        in_specs=[smem_spec()] + far_specs(1),
        out_specs=tuple(vmem_specs(4)),
        scratch_shapes=[pltpu.VMEM(state.shape, F32)]
        + [pltpu.VMEM(edge, F32)] * 2
        + [pltpu.SemaphoreType.DMA((2,))],
        compiler_params=params(8),
        name="turn_state",
    )(place, *in_hbm(state))


def framed_row(place_ref, own_ref, near_ref, far_ref, r, cells, held=None):
    at = pl.ds(r * SIDE, SIDE)
    near = near_ref[at, :].astype(F32)
    far = far_ref[at, :].astype(F32)
    own = own_ref[pl.ds((r if held is None else held) * cells, cells), :].astype(F32)
    left = either(place_ref[0], far, near)
    right = either(place_ref[0], near, far)
    return jnp.concatenate([left, own, right], axis=0)


def frame_kernel(place_ref, own_ref, lon_near_ref, lon_far_ref, near_ref, far_ref):
    rows = lon_near_ref.shape[0] // SIDE
    cells = own_ref.shape[0] // (2 * HALO)
    width = cells + 2 * SIDE
    for i in range(HALO):
        top = framed_row(place_ref, own_ref, lon_near_ref, lon_far_ref, i, cells, i)
        low = framed_row(place_ref, own_ref, lon_near_ref, lon_far_ref, rows - HALO + i, cells, HALO + i)
        at = pl.ds(i * width, width)
        near_ref[at, :] = either(place_ref[1], low, top).astype(BF16)
        far_ref[at, :] = either(place_ref[1], top, low).astype(BF16)


def frame_rows(place, own, lon_near, lon_far, width):
    shape = (HALO * width, own.shape[1])
    return pl.pallas_call(
        frame_kernel,
        out_shape=(jax.ShapeDtypeStruct(shape, BF16),) * 2,
        in_specs=[smem_spec()] + vmem_specs(3),
        out_specs=tuple(vmem_specs(2)),
        compiler_params=params(8),
        name="frame_rows",
    )(place, own, lon_near, lon_far)


def weight_scratch(weights):
    return [pltpu.VMEM(weight.shape, BF16) for weight in weights]


def forward_kernel(
    place_ref, own_ref, lon_near_ref, lon_far_ref, lat_near_ref, lat_far_ref, op_ref, w0_far, wm_far, w3_far,
    pre_far, pred_ref, edge_ref, d0_far, d1_far, d2_far,
    buf_a, buf_b, acc_a, acc_b, w0, wm, w3, pre_ref, clean_a, clean_b, d0, d1, d2, in_sems, out_sems,
):
    rows, width, channels = pre_ref.shape
    cells = width - 2 * SIDE
    weights = (w0, wm.at[0], wm.at[1], w3)
    slopes = (d0, d1, d2)
    loads = copies(
        ((w0_far, w0), (wm_far.at[0], wm.at[0]), (wm_far.at[1], wm.at[1]), (w3_far, w3)), in_sems
    )
    stores = copies(((d0, d0_far), (d1, d1_far), (d2, d2_far), (pre_ref, pre_far)), out_sems)
    for load in loads:
        load.start()

    def fill(i, carry):
        put_shifted(buf_a, i + HALO, width, framed_row(place_ref, own_ref, lon_near_ref, lon_far_ref, i, cells))
        return carry

    lax.fori_loop(0, rows, fill, 0)
    for i in range(HALO):
        at = pl.ds(i * width, width)
        near = lat_near_ref[at, :].astype(F32)
        far = lat_far_ref[at, :].astype(F32)
        put_shifted(buf_a, i, width, either(place_ref[1], far, near))
        put_shifted(buf_a, i + HALO + rows, width, either(place_ref[1], near, far))
    src, dst = buf_a, buf_b
    for layer in range(LAYERS):
        margin = HALO - 1 - layer
        count = rows + 2 * margin

        def compute(row, n, src=src, layer=layer):
            return conv_block(src, row, n, width, weights[layer], 0 if layer == 0 else 1, False)

        loads[layer].wait()

        if layer < LAYERS - 1:

            def finish(row, n, value, dst=dst, layer=layer):
                gate = 0.5 + 0.5 * jnp.tanh(0.5 * value)
                act = value * gate
                slope = gate + act * (1.0 - gate)
                slopes[layer][pl.ds(row * width, n * width), :] = slope.astype(BF16)
                put_shifted(dst, row, width, act)

        else:

            def finish(row, n, value):
                for i in range(n):
                    part = value[i * width : (i + 1) * width, :]
                    pre_ref[row + i] = part
                    own = framed_row(place_ref, own_ref, lon_near_ref, lon_far_ref, row + i, cells)
                    clean = (own + part).astype(BF16)
                    at = pl.ds((row + i) * width, width)
                    clean_a[at, :] = clean[:, 0:128].astype(F32)
                    clean_b[at, 0 : channels - 128] = clean[:, 128:channels].astype(F32)
                    pred_ref[row + i] = lax.dot_general(
                        op_ref[:, 0:channels],
                        clean[SIDE : SIDE + cells, :],
                        (((1,), (1,)), ((), ())),
                        preferred_element_type=F32,
                    )

        conv_layer(count, compute, finish, acc_a, acc_b)
        if layer < LAYERS - 1:
            size = margin * width

            def clear(first, dst=dst, layer=layer, size=size):
                slopes[layer][first : first + size, :] = jnp.zeros((size, LANES), BF16)
                dst[first : first + size, :] = jnp.zeros((size, 3 * LANES), BF16)

            @pl.when(place_ref[2] == 1)
            def _():
                clear(0)

            @pl.when(place_ref[3] == 1)
            def _(count=count, size=size):
                clear(count * width - size)

        stores[layer].start()
        src, dst = dst, src
    tall = jnp.concatenate([op_ref[:, 0:channels].astype(F32), jnp.zeros((96, channels), F32)], axis=0).astype(BF16)
    for end, first in ((0, SIDE - EDGE), (1, SIDE + cells)):
        total = None
        for c in range(EDGE):
            at = pl.ds(first + c, rows, stride=width)
            clean = jnp.concatenate([clean_a[at, :], clean_b[at, :]], axis=1)[:, 0:channels]
            part = lax.dot_general(
                clean.astype(BF16), tall, (((1,), (1,)), ((), ())), preferred_element_type=F32
            )
            part = pltpu.roll(part, c * SLOT, 1) if c else part
            total = part if total is None else total + part
        edge_ref[end] = total
    for store in stores:
        store.wait()


def forward_pass(place, own, lon, lat, weights, operator, rows, width):
    slopes = [((rows + 2 * (HALO - 1 - layer)) * width, LANES) for layer in range(LAYERS - 1)]
    pre = (rows, width, own.shape[1])
    padded = (rows + 2 * HALO) * width
    return pl.pallas_call(
        forward_kernel,
        out_shape=(
            pltpu.HBM(pre, F32),
            pltpu.HBM((rows, operator.shape[0], width - 2 * SIDE), F32),
            pltpu.HBM((2, rows, 128), F32),
        )
        + tuple(pltpu.HBM(shape, BF16) for shape in slopes),
        in_specs=[smem_spec()] + vmem_specs(6) + far_specs(3),
        out_specs=tuple(far_specs(1) + vmem_specs(2) + far_specs(3)),
        scratch_shapes=[pltpu.VMEM((padded, 3 * LANES), BF16)] * 2
        + [pltpu.VMEM((BLOCK * width, LANES), F32)] * 2
        + weight_scratch(weights)
        + [pltpu.VMEM(pre, F32)] + [pltpu.VMEM((rows * width, 128), F32)] * 2
        + [pltpu.VMEM(shape, BF16) for shape in slopes]
        + [pltpu.SemaphoreType.DMA((LAYERS,)), pltpu.SemaphoreType.DMA((LAYERS,))],
        compiler_params=params(34),
        name="forward_pass",
    )(place, *in_hbm(own), *lon, *lat, operator, *in_hbm(*weights))


LEAD = HALO + 1


def slope_rows(layer, first):
    return first - (layer - HALO + 1)


def edge_kernel(
    place_ref, recv_ref, pred_ref, pred_edge_ref, op_ref, prec_ref, prec_edge_ref,
    d0_far, d1_far, d2_far, w0_far, wm_far, w3_far,
    pulled_ref, near_ref, far_ref, s0_ref, s1_ref, s2_ref,
    wide_ref, sums_ref, field_a, field_b, buf_a, buf_b, acc_a, acc_b, w0, wm, w3, d_ref, in_sems,
):
    rows, cells, channels = pred_ref.shape[0], pred_ref.shape[2], near_ref.shape[1]
    width = cells + 2 * SIDE
    slots = recv_ref.shape[0] // SLOT
    weights = (w0, wm.at[0], wm.at[1], w3)
    strips = (s0_ref, s1_ref, s2_ref)
    size = HALO * width
    pairs = [(w3_far, w3), (wm_far.at[1], wm.at[1]), (wm_far.at[0], wm.at[0]), (w0_far, w0)]
    for layer, source in ((2, d2_far), (1, d1_far), (0, d0_far)):
        for end in range(2):
            first = layer + 1 - HALO if end == 0 else rows - 1 - layer
            at = slope_rows(layer, first) * width
            pairs.append((source.at[pl.ds(at, size)], d_ref.at[layer, end]))
    loads = copies(pairs, in_sems)
    for load in loads:
        load.start()

    nothing = jnp.zeros((4 * width, 3 * LANES), BF16)
    buf_a[width : 5 * width, :] = nothing
    buf_a[(rows + 5) * width : (rows + 9) * width, :] = nothing
    buf_b[0 : 4 * width, :] = nothing
    buf_b[(rows + 6) * width : (rows + 10) * width, :] = nothing

    wide_ref[...] = recv_ref[...].astype(F32)
    sums_ref[...] = jnp.zeros(sums_ref.shape, F32)
    sides = [wide_ref[pl.ds(BANDS + end, slots, stride=SLOT), :] for end in range(2)]
    lane = lax.broadcasted_iota(jnp.int32, (slots, cells), 1).astype(F32)
    own = sides[0][:, BANDS + 1 : BANDS + 2]
    before = sides[0][:, BANDS : BANDS + 1] + rows
    after = sides[1][:, BANDS : BANDS + 1] + 2 * rows
    wanted = jnp.where(lane < rows, own, jnp.where(lane < 2 * rows, before, after))
    least = jnp.where(lane < rows, 0.0, jnp.where(lane < 2 * rows, 1.0 * rows, 2.0 * rows))
    match = (wanted == lane + 1.0) & (wanted > least) & (lane < 3 * rows)
    onehot = jnp.transpose(match.astype(F32))[0 : 3 * rows, :].astype(BF16)
    held = jnp.dot(onehot, jnp.ones((slots, cells), BF16), preferred_element_type=F32)
    own_hot = onehot[0:rows, :]
    for k in range(BANDS):
        part = wide_ref[pl.ds(k, slots, stride=SLOT), :].astype(BF16)
        sums_ref[pl.ds(k, rows, stride=32), :] = jnp.dot(own_hot, part, preferred_element_type=F32)
    nothing = jnp.zeros((SIDE, 128), F32)
    for r in range(rows):
        summed = sums_ref[r * 32 : (r + 1) * 32, :]
        weighted = (summed - held[r : r + 1, :] * pred_ref[r]) * prec_ref[...]
        at = r * width
        value = jnp.dot(
            jnp.transpose(weighted).astype(BF16), op_ref[...], preferred_element_type=F32
        )
        for field, part in ((field_a, value[:, 0:128]), (field_b, value[:, 128:LANES])):
            field[at : at + SIDE, :] = nothing
            field[at + SIDE : at + SIDE + cells, :] = part
            field[at + SIDE + cells : at + width, :] = nothing
    short = op_ref[...].astype(F32)[0:SLOT, :]
    for end, first in ((0, SIDE - EDGE), (1, SIDE + cells)):
        part = onehot[(1 + end) * rows : (2 + end) * rows, :]
        summed = jnp.dot(part, sides[end].astype(BF16), preferred_element_type=F32)
        count = held[(1 + end) * rows : (2 + end) * rows, :]
        weighted = ((summed - count * pred_edge_ref[end]) * prec_edge_ref[...]).astype(BF16)
        for c in range(EDGE):
            above = [jnp.zeros((c * SLOT, LANES), F32)] if c else []
            below = jnp.zeros((128 - (c + 1) * SLOT, LANES), F32)
            picked = jnp.concatenate(above + [short, below], axis=0).astype(BF16)
            value = jnp.dot(weighted, picked, preferred_element_type=F32)
            at = pl.ds(first + c, rows, stride=width)
            field_a[at, :] = value[:, 0:128]
            field_b[at, :] = value[:, 128:LANES]
    for r in range(rows):
        at = slice(r * width, (r + 1) * width)
        row = jnp.concatenate([field_a[at, :], field_b[at, :]], axis=1)[:, 0:channels]
        pulled_ref[r] = row
        if r < HALO or r >= rows - HALO:
            put_shifted(buf_a, r + LEAD, width, row)

    src, dst = buf_a, buf_b
    for layer in range(LAYERS - 1, -1, -1):
        margin = LAYERS - layer
        tops = (-margin, rows + margin - HALO)
        accs = (acc_a, acc_b)
        loads[LAYERS - 1 - layer].wait()
        for end in range(2):
            value = conv_block(
                src, tops[end] + LEAD - 1, HALO, width, weights[layer], 1 if layer == 0 else 0, True
            )
            accs[end][:, 0 : value.shape[1]] = value
        if layer > 0:
            for end in range(2):
                loads[LAYERS + 2 * (LAYERS - 1 - layer) + end].wait()
                value = accs[end][...] * d_ref[layer - 1, end].astype(F32)
                put_shifted(dst, tops[end] + LEAD, width, value)
                half = size // 2
                kept = value[half:, :] if end == 0 else value[0:half, :]
                strips[layer - 1][end * half : (end + 1) * half, :] = kept.astype(BF16)
        else:
            for i in range(HALO):
                at = slice(i * width + SIDE, i * width + SIDE + cells)
                top = acc_a[at, 0:channels]
                low = acc_b[at, 0:channels]
                near_ref[i] = jnp.transpose(either(place_ref[1], low, top)).astype(BF16)
                far_ref[i] = jnp.transpose(either(place_ref[1], top, low)).astype(BF16)
        src, dst = dst, src


def edge_pass(place, recv, pred, pred_edge, slopes, operator, precision, precision_edge, weights, channels):
    rows, cells = pred.shape[0], pred.shape[2]
    width = cells + 2 * SIDE
    padded = (rows + 2 * LEAD) * width
    size = HALO * width
    return pl.pallas_call(
        edge_kernel,
        out_shape=(
            pltpu.HBM((rows, width, channels), F32),
            jax.ShapeDtypeStruct((HALO, channels, cells), BF16),
            jax.ShapeDtypeStruct((HALO, channels, cells), BF16),
        )
        + tuple(pltpu.HBM((size, LANES), BF16) for _ in range(LAYERS - 1)),
        in_specs=[smem_spec()] + vmem_specs(6) + far_specs(6),
        out_specs=tuple(vmem_specs(6)),
        scratch_shapes=[
            pltpu.VMEM(recv.shape, F32),
            pltpu.VMEM((rows * 32, recv.shape[1]), F32),
            pltpu.VMEM((rows * width, 128), F32),
            pltpu.VMEM((rows * width, 128), F32),
        ]
        + [pltpu.VMEM((padded, 3 * LANES), BF16)] * 2
        + [pltpu.VMEM((size, LANES), F32)] * 2
        + weight_scratch(weights)
        + [pltpu.VMEM((LAYERS - 1, 2, size, LANES), BF16), pltpu.SemaphoreType.DMA((LAYERS + 6,))],
        compiler_params=params(34),
        name="edge_pass",
    )(place, recv, *in_hbm(pred, pred_edge), operator, precision, precision_edge, *in_hbm(*slopes, *weights))


def inner_kernel(
    level_ref, step_ref, pulled_ref, s0_ref, s1_ref, s2_ref,
    pre_far, d0_far, d1_far, d2_far, w0_far, wm_far, w3_far, state_far, noise_far,
    base_ref,
    buf_a, buf_b, acc_a, acc_b, w0, wm, w3, pre_ref, d0, d1, d2, state_ref, noise_ref, in_sems,
):
    rows, width, _ = pulled_ref.shape
    cells = width - 2 * SIDE
    level = jnp.full((1, 128), level_ref[0], F32)
    inverse = (1.0 / (level * level))[:, 0:1]
    step = jnp.full((1, 128), step_ref[0], F32)
    spread = jnp.sqrt(2.0 * step)
    weights = (w0, wm.at[0], wm.at[1], w3)
    strips = (s0_ref, s1_ref, s2_ref)
    slopes = (d0, d1, d2)
    pairs = [(w3_far, w3)]
    for layer, source, weight in ((2, d2_far, 1), (1, d1_far, 0), (0, d0_far, None)):
        first = layer + 1
        count = slopes[layer].shape[0]
        pairs.append((source.at[pl.ds(slope_rows(layer, first) * width, count)], slopes[layer]))
        pairs.append((w0_far, w0) if weight is None else (wm_far.at[weight], wm.at[weight]))
    pairs += [(pre_far, pre_ref), (state_far, state_ref), (noise_far, noise_ref)]
    loads = copies(pairs, in_sems)
    for load in loads:
        load.start()

    def fill(r, carry):
        put_shifted(buf_a, r + LEAD, width, pulled_ref[r])
        return carry

    lax.fori_loop(0, rows, fill, 0)
    loads[0].wait()
    src, dst = buf_a, buf_b
    half = HALO // 2 * width
    for layer in range(LAYERS - 1, -1, -1):
        begin = layer
        count = rows - 2 * layer

        def compute(row, n, src=src, layer=layer, begin=begin):
            return conv_block(
                src, row + begin + LEAD - 1, n, width, weights[layer], 1 if layer == 0 else 0, True
            )

        if layer > 0:
            kept = strips[layer - 1]
            put_shifted(dst, layer - 2 + LEAD, width, kept[0:half, :].astype(F32))
            put_shifted(dst, rows - layer + LEAD, width, kept[half:, :].astype(F32))
            loads[2 * (LAYERS - 1 - layer) + 1].wait()

            def finish(row, n, value, dst=dst, layer=layer, begin=begin):
                slope = slopes[layer - 1][pl.ds(row * width, n * width), :]
                put_shifted(dst, row + begin + LEAD, width, value * slope.astype(F32))

            conv_layer(count, compute, finish, acc_a, acc_b)
            loads[2 * (LAYERS - 1 - layer) + 2].wait()
        else:
            for load in loads[-3:]:
                load.wait()

            def finish(row, n, value):
                for i in range(n):
                    total = pre_ref[row + i] * inverse + pulled_ref[row + i] + value[i * width : (i + 1) * width, :]
                    turned = jnp.transpose(total[SIDE : SIDE + cells, :])
                    r = row + i
                    base_ref[:, r, :] = state_ref[:, r, :] + step * turned + spread * noise_ref[:, r, :]

            conv_layer(count, compute, finish, acc_a, acc_b)
        src, dst = dst, src


def inner_pass(level, step, pulled, strips, pre, slopes, weights, state, noise):
    rows, width, _ = pre.shape
    padded = (rows + 2 * LEAD) * width
    kept = [((rows - 2 * (layer + 1)) * width, LANES) for layer in range(LAYERS - 1)]
    return pl.pallas_call(
        inner_kernel,
        out_shape=jax.ShapeDtypeStruct(state.shape, F32),
        in_specs=[smem_spec(), smem_spec()] + vmem_specs(4) + far_specs(9),
        out_specs=vmem_specs(1)[0],
        scratch_shapes=[pltpu.VMEM((padded, 3 * LANES), BF16)] * 2
        + [pltpu.VMEM((BLOCK * width, LANES), F32)] * 2
        + weight_scratch(weights)
        + [pltpu.VMEM(pre.shape, F32)]
        + [pltpu.VMEM(shape, BF16) for shape in kept]
        + [pltpu.VMEM(state.shape, F32)] * 2
        + [pltpu.SemaphoreType.DMA((2 * LAYERS + 2,))],
        compiler_params=params(34),
        name="inner_pass",
    )(level, step, *in_hbm(pulled, *strips, pre, *slopes, *weights, state, noise))


def final_kernel(place_ref, step_ref, base_ref, near_ref, far_ref, out_ref):
    rows = base_ref.shape[1]
    step = jnp.full((1, 128), step_ref[0], F32)
    out_ref[...] = base_ref[...]
    for i in range(HALO):
        near = near_ref[i].astype(F32)
        far = far_ref[i].astype(F32)
        r = rows - HALO + i
        out_ref[:, i, :] = base_ref[:, i, :] + step * either(place_ref[1], far, near)
        out_ref[:, r, :] = base_ref[:, r, :] + step * either(place_ref[1], near, far)


def final_pass(place, step, base, near, far):
    return pl.pallas_call(
        final_kernel,
        out_shape=jax.ShapeDtypeStruct(base.shape, F32),
        in_specs=[smem_spec(), smem_spec()] + vmem_specs(3),
        out_specs=vmem_specs(1)[0],
        compiler_params=params(8),
        name="final_pass",
    )(place, step, base, near, far)


def swap_pairs(size, first, wrap):
    pairs = []
    for low in range(first, size if wrap else size - 1, 2):
        high = (low + 1) % size
        pairs += [(low, high), (high, low)]
    return pairs


def swap(axis, wrap, near, far):
    size = lax.axis_size(axis)
    return lax.ppermute(near, axis, swap_pairs(size, 0, wrap)), lax.ppermute(far, axis, swap_pairs(size, 1, wrap))


def pad_to(values, shape):
    return jnp.pad(values, [(0, n - m) for m, n in zip(values.shape, shape)])


def shards(
    state,
    noise,
    first_kernel,
    middle_kernels,
    last_kernel,
    obs_values,
    obs_holder,
    obs_tile,
    obs_operator,
    obs_precision,
    noise_level,
    step_size,
):
    channels, rows, cells = state.shape
    width = cells + 2 * SIDE
    weights = (jnp.transpose(first_kernel, (0, 2, 1)), middle_kernels, last_kernel)
    lon, lat = lax.axis_index("lon"), lax.axis_index("lat")
    bands = lax.axis_size("lat")
    place = jnp.stack([lon % 2 == 0, lat % 2 == 0, lat == 0, lat == bands - 1]).astype(jnp.int32)

    holders = lax.axis_size(("lon", "lat"))
    packed = pack_blocks(obs_holder, obs_tile, obs_values, holders * CAPACITY, bands * CAPACITY)
    own, outer, *edges = turn_state(place, state)
    lon_halo = swap("lon", True, *edges)
    framed = frame_rows(place, outer, *lon_halo, width)
    packed, framed = lax.optimization_barrier((packed, framed))
    lat_halo = swap("lat", False, *framed)
    recv = lax.all_to_all(
        packed.reshape(holders, CAPACITY * SLOT, cells), ("lon", "lat"), split_axis=0, concat_axis=0, tiled=True
    ).reshape(packed.shape)

    operator = pad_to(obs_operator, (32, LANES))
    precision = pad_to(obs_precision[:, None], (32, 1))
    precision_edge = pad_to(jnp.tile(pad_to(obs_precision, (SLOT,)), EDGE)[None, :], (1, 128))
    pre, pred, pred_edge, *slopes = forward_pass(place, own, lon_halo, lat_halo, weights, operator, rows, width)
    pulled, near, far, *strips = edge_pass(
        place, recv, pred, pred_edge, slopes, operator, precision, precision_edge, weights, channels
    )
    near, far = swap("lat", False, near, far)
    base = inner_pass(noise_level, step_size, pulled, strips, pre, slopes, weights, state, noise)
    return final_pass(place, step_size, base, near, far)


def solution(mesh):
    placed = (
        P(None, "lat", "lon"),
        P(None, "lat", "lon"),
        P(),
        P(),
        P(),
        P(("lon", "lat"), None, None),
        P(("lon", "lat"), None),
        P(("lon", "lat")),
        P(),
        P(),
        P(),
        P(),
    )

    return jax.shard_map(
        shards, mesh=mesh, in_specs=placed, out_specs=P(None, "lat", "lon"), check_vma=False
    )
```

```python
import functools

import jax
import jax.numpy as jnp
from jax import lax
from jax.experimental import pallas as pl
from jax.experimental.pallas import tpu as pltpu
from jax.sharding import PartitionSpec as P


LAYERS = 4
CAPACITY = 2
HALO = 4
SIDE = 8
LANES = 256
SLOT = 24
BLOCK = 4
F32 = jnp.float32
BF16 = jnp.bfloat16


def vmem_specs(count):
    return [pl.BlockSpec(memory_space=pltpu.VMEM) for _ in range(count)]


def smem_spec():
    return pl.BlockSpec(memory_space=pltpu.SMEM)


def params(mebibytes):
    return pltpu.CompilerParams(vmem_limit_bytes=mebibytes << 20)


def in_hbm(*arrays):
    return [pltpu.with_memory_space_constraint(array, pltpu.HBM) for array in arrays]


def far_specs(count):
    return [pl.BlockSpec(memory_space=pl.ANY) for _ in range(count)]


def copies(pairs, sems):
    return [pltpu.make_async_copy(src, dst, sems.at[i]) for i, (src, dst) in enumerate(pairs)]


BANDS = 22
EDGE = 4


def pack_kernel(holder_ref, tile_ref, values_ref, out_ref, wide_ref, *, shift):
    count, width = values_ref.shape[1], values_ref.shape[2]
    slots = out_ref.shape[0] // SLOT
    named = jnp.broadcast_to(holder_ref[...].astype(F32), (count, count))
    first = lax.broadcasted_iota(jnp.int32, (count, count), 0)
    second = lax.broadcasted_iota(jnp.int32, (count, count), 1)
    same = (jnp.transpose(named) == named) & (first < second)
    ranks = jnp.sum(same.astype(F32), axis=0, keepdims=True)
    chosen = holder_ref[...] * CAPACITY + ranks.astype(jnp.int32)
    onehot = lax.broadcasted_iota(jnp.int32, (slots, count), 0) == chosen
    onehot = onehot.astype(F32).astype(BF16)
    numbers = jnp.broadcast_to((tile_ref[...] + 1).astype(F32), (width, count))
    numbers = jnp.transpose(numbers).astype(BF16)
    cell = lax.broadcasted_iota(jnp.int32, (width, 2 * width), 0)
    lane = lax.broadcasted_iota(jnp.int32, (width, 2 * width), 1)
    high = lane - (cell - (width - EDGE)) * SLOT
    low = lane - width - cell * SLOT
    channel = jnp.where(
        lane < width, jnp.where(cell >= width - EDGE, high, -1), jnp.where(cell < EDGE, low, -1)
    )
    edges = None
    for k in range(BANDS + 1):
        values = values_ref[k] if k < BANDS else numbers
        if k < BANDS:
            wide_ref[pl.ds(k, slots, stride=SLOT), :] = jnp.dot(
                onehot, values, preferred_element_type=F32
            )
        spread = (channel == k).astype(F32).astype(BF16)
        part = jnp.dot(values, spread, preferred_element_type=F32)
        edges = part if edges is None else edges + part
    placed = jnp.dot(onehot, edges.astype(BF16), preferred_element_type=F32)
    own = jnp.dot(onehot, numbers, preferred_element_type=F32)
    before = pltpu.roll(placed[:, 0:width], shift, 0)
    after = pltpu.roll(placed[:, width : 2 * width], slots - shift, 0)
    at = lax.broadcasted_iota(jnp.int32, (slots, width), 1)
    wide_ref[pl.ds(BANDS, slots, stride=SLOT), :] = jnp.where(at == BANDS + 1, own, before)
    wide_ref[pl.ds(BANDS + 1, slots, stride=SLOT), :] = after
    out_ref[...] = wide_ref[0 : slots * SLOT, :].astype(BF16)


def pack_blocks(holders, tiles, values, slot_count, shift):
    width = values.shape[2]
    return pl.pallas_call(
        functools.partial(pack_kernel, shift=shift),
        out_shape=jax.ShapeDtypeStruct((slot_count * SLOT, width), BF16),
        in_specs=vmem_specs(3),
        out_specs=vmem_specs(1)[0],
        scratch_shapes=[pltpu.VMEM(((slot_count + 1) * SLOT, width), F32)],
        compiler_params=params(12),
        name="pack_blocks",
    )(*in_hbm(holders.reshape(1, -1), tiles.reshape(1, -1), jnp.transpose(values, (1, 0, 2))))


def put_shifted(dst_ref, row, width, act):
    size, channels = act.shape
    at = pl.ds(row * width, size)
    dst_ref[at, LANES : LANES + channels] = act.astype(BF16)
    dst_ref[at, 0:channels] = pltpu.roll(act, 1, 0).astype(BF16)
    dst_ref[at, 2 * LANES : 2 * LANES + channels] = pltpu.roll(act, size - 1, 0).astype(BF16)


def conv_block(src_ref, row, rows, width, w_ref, side, flip):
    acc = None
    taken = w_ref.shape[1 + side]
    for p in range(3):
        at = pl.ds((row + p) * width, rows * width)
        for q in range(3):
            tap = 3 * p + q
            part = lax.dot_general(
                src_ref[at, q * LANES : q * LANES + taken],
                w_ref[8 - tap if flip else tap],
                (((1,), (side,)), ((), ())),
                preferred_element_type=F32,
            )
            acc = part if acc is None else acc + part
    return acc


def conv_layer(rows, compute, finish, acc_a, acc_b):
    full, rest = divmod(rows, BLOCK)
    first = compute(0, BLOCK)
    size, channels = first.shape
    unit = size // BLOCK

    def keep(acc, value):
        acc[0 : value.shape[0], 0:channels] = value

    def kept(acc, n):
        return acc[0 : n * unit, 0:channels]

    keep(acc_a, first)
    pairs = (full - 1) // 2

    def body(j, carry):
        row = 2 * BLOCK * j
        keep(acc_b, compute(row + BLOCK, BLOCK))
        finish(row, BLOCK, kept(acc_a, BLOCK))
        keep(acc_a, compute(row + 2 * BLOCK, BLOCK))
        finish(row + BLOCK, BLOCK, kept(acc_b, BLOCK))
        return carry

    if pairs > 1:
        lax.fori_loop(0, pairs, body, 0)
    elif pairs:
        body(0, 0)
    done = 2 * pairs
    last, free = acc_a, acc_b
    if full - 1 > done:
        keep(acc_b, compute((done + 1) * BLOCK, BLOCK))
        finish(done * BLOCK, BLOCK, kept(acc_a, BLOCK))
        last, free = acc_b, acc_a
    if rest:
        keep(free, compute(full * BLOCK, rest))
    finish((full - 1) * BLOCK, BLOCK, kept(last, BLOCK))
    if rest:
        finish(full * BLOCK, rest, kept(free, rest))


def either(flag, yes, no):
    return jnp.where(flag == 1, yes, no)


def turn_kernel(
    place_ref, state_far, own_ref, outer_ref, near_ref, far_ref, state_ref, low_ref, high_ref, sems
):
    _, rows, cells = state_ref.shape
    half = rows // 2
    parts = [pl.ds(0, half), pl.ds(half, half)]
    loads = copies([(state_far.at[:, at, :], state_ref.at[:, at, :]) for at in parts], sems)
    for load in loads:
        load.start()
    for r in range(rows):
        if r % half == 0:
            loads[r // half].wait()
        part = jnp.transpose(state_ref[:, r, :])
        turned = part.astype(BF16)
        own_ref[r * cells : (r + 1) * cells, :] = turned
        if r < HALO or r >= rows - HALO:
            at = outer_row(r, rows) * cells
            outer_ref[at : at + cells, :] = turned
        low_ref[r * SIDE : (r + 1) * SIDE, :] = part[0:SIDE, :]
        high_ref[r * SIDE : (r + 1) * SIDE, :] = part[cells - SIDE : cells, :]
    low = low_ref[...]
    high = high_ref[...]
    near_ref[...] = either(place_ref[0], high, low).astype(BF16)
    far_ref[...] = either(place_ref[0], low, high).astype(BF16)


def outer_row(r, rows):
    return r if r < HALO else r - (rows - HALO) + HALO


def turn_state(place, state):
    channels, rows, cells = state.shape
    edge = (rows * SIDE, channels)
    return pl.pallas_call(
        turn_kernel,
        out_shape=(
            pltpu.HBM((rows * cells, channels), BF16),
            jax.ShapeDtypeStruct((2 * HALO * cells, channels), BF16),
            jax.ShapeDtypeStruct(edge, BF16),
            jax.ShapeDtypeStruct(edge, BF16),
        ),
        in_specs=[smem_spec()] + far_specs(1),
        out_specs=tuple(vmem_specs(4)),
        scratch_shapes=[pltpu.VMEM(state.shape, F32)]
        + [pltpu.VMEM(edge, F32)] * 2
        + [pltpu.SemaphoreType.DMA((2,))],
        compiler_params=params(8),
        name="turn_state",
    )(place, *in_hbm(state))


def framed_row(place_ref, own_ref, near_ref, far_ref, r, cells, held=None):
    at = pl.ds(r * SIDE, SIDE)
    near = near_ref[at, :].astype(F32)
    far = far_ref[at, :].astype(F32)
    own = own_ref[pl.ds((r if held is None else held) * cells, cells), :].astype(F32)
    left = either(place_ref[0], far, near)
    right = either(place_ref[0], near, far)
    return jnp.concatenate([left, own, right], axis=0)


def frame_kernel(place_ref, own_ref, lon_near_ref, lon_far_ref, near_ref, far_ref):
    rows = lon_near_ref.shape[0] // SIDE
    cells = own_ref.shape[0] // (2 * HALO)
    width = cells + 2 * SIDE
    for i in range(HALO):
        top = framed_row(place_ref, own_ref, lon_near_ref, lon_far_ref, i, cells, i)
        low = framed_row(place_ref, own_ref, lon_near_ref, lon_far_ref, rows - HALO + i, cells, HALO + i)
        at = pl.ds(i * width, width)
        near_ref[at, :] = either(place_ref[1], low, top).astype(BF16)
        far_ref[at, :] = either(place_ref[1], top, low).astype(BF16)


def frame_rows(place, own, lon_near, lon_far, width):
    shape = (HALO * width, own.shape[1])
    return pl.pallas_call(
        frame_kernel,
        out_shape=(jax.ShapeDtypeStruct(shape, BF16),) * 2,
        in_specs=[smem_spec()] + vmem_specs(3),
        out_specs=tuple(vmem_specs(2)),
        compiler_params=params(8),
        name="frame_rows",
    )(place, own, lon_near, lon_far)


def weight_scratch(weights):
    return [pltpu.VMEM(weight.shape, BF16) for weight in weights]


def forward_kernel(
    place_ref, own_ref, lon_near_ref, lon_far_ref, lat_near_ref, lat_far_ref, op_ref, w0_far, wm_far, w3_far,
    pre_far, pred_ref, edge_ref, d0_far, d1_far, d2_far,
    buf_a, buf_b, acc_a, acc_b, w0, wm, w3, pre_ref, clean_a, clean_b, d0, d1, d2, in_sems, out_sems,
):
    rows, width, channels = pre_ref.shape
    cells = width - 2 * SIDE
    weights = (w0, wm.at[0], wm.at[1], w3)
    slopes = (d0, d1, d2)
    loads = copies(
        ((w0_far, w0), (wm_far.at[0], wm.at[0]), (wm_far.at[1], wm.at[1]), (w3_far, w3)), in_sems
    )
    stores = copies(((d0, d0_far), (d1, d1_far), (d2, d2_far)), out_sems)
    for load in loads:
        load.start()

    def fill(i, carry):
        put_shifted(buf_a, i + HALO, width, framed_row(place_ref, own_ref, lon_near_ref, lon_far_ref, i, cells))
        return carry

    lax.fori_loop(0, rows, fill, 0)
    for i in range(HALO):
        at = pl.ds(i * width, width)
        near = lat_near_ref[at, :].astype(F32)
        far = lat_far_ref[at, :].astype(F32)
        put_shifted(buf_a, i, width, either(place_ref[1], far, near))
        put_shifted(buf_a, i + HALO + rows, width, either(place_ref[1], near, far))
    src, dst = buf_a, buf_b
    for layer in range(LAYERS):
        margin = HALO - 1 - layer
        count = rows + 2 * margin

        def compute(row, n, src=src, layer=layer):
            return conv_block(src, row, n, width, weights[layer], 0 if layer == 0 else 1, False)

        loads[layer].wait()

        if layer < LAYERS - 1:

            def finish(row, n, value, dst=dst, layer=layer):
                gate = 0.5 + 0.5 * jnp.tanh(0.5 * value)
                act = value * gate
                slope = gate + act * (1.0 - gate)
                slopes[layer][pl.ds(row * width, n * width), :] = slope.astype(BF16)
                put_shifted(dst, row, width, act)

        else:

            def finish(row, n, value):
                for i in range(n):
                    part = value[i * width : (i + 1) * width, :]
                    pre_ref[row + i] = part
                    own = framed_row(place_ref, own_ref, lon_near_ref, lon_far_ref, row + i, cells)
                    clean = (own + part).astype(BF16)
                    at = pl.ds((row + i) * width, width)
                    clean_a[at, :] = clean[:, 0:128].astype(F32)
                    clean_b[at, 0 : channels - 128] = clean[:, 128:channels].astype(F32)
                    pred_ref[row + i] = lax.dot_general(
                        op_ref[:, 0:channels],
                        clean[SIDE : SIDE + cells, :],
                        (((1,), (1,)), ((), ())),
                        preferred_element_type=F32,
                    )
                at = pl.ds(row, n)
                store = pltpu.make_async_copy(
                    pre_ref.at[at], pre_far.at[at], out_sems.at[LAYERS - 1 + row // BLOCK]
                )
                store.start()
                stores.append(store)

        conv_layer(count, compute, finish, acc_a, acc_b)
        if layer < LAYERS - 1:
            size = margin * width

            def clear(first, dst=dst, layer=layer, size=size):
                slopes[layer][first : first + size, :] = jnp.zeros((size, LANES), BF16)
                dst[first : first + size, :] = jnp.zeros((size, 3 * LANES), BF16)

            @pl.when(place_ref[2] == 1)
            def _():
                clear(0)

            @pl.when(place_ref[3] == 1)
            def _(count=count, size=size):
                clear(count * width - size)

        if layer < LAYERS - 1:
            stores[layer].start()
        src, dst = dst, src
    tall = jnp.concatenate([op_ref[:, 0:channels].astype(F32), jnp.zeros((96, channels), F32)], axis=0).astype(BF16)
    for end, first in ((0, SIDE - EDGE), (1, SIDE + cells)):
        total = None
        for c in range(EDGE):
            at = pl.ds(first + c, rows, stride=width)
            clean = jnp.concatenate([clean_a[at, :], clean_b[at, :]], axis=1)[:, 0:channels]
            part = lax.dot_general(
                clean.astype(BF16), tall, (((1,), (1,)), ((), ())), preferred_element_type=F32
            )
            part = pltpu.roll(part, c * SLOT, 1) if c else part
            total = part if total is None else total + part
        edge_ref[end] = total
    for store in stores:
        store.wait()


def forward_pass(place, own, lon, lat, weights, operator, rows, width):
    slopes = [((rows + 2 * (HALO - 1 - layer)) * width, LANES) for layer in range(LAYERS - 1)]
    pre = (rows, width, own.shape[1])
    padded = (rows + 2 * HALO) * width
    return pl.pallas_call(
        forward_kernel,
        out_shape=(
            pltpu.HBM(pre, F32),
            pltpu.HBM((rows, operator.shape[0], width - 2 * SIDE), F32),
            pltpu.HBM((2, rows, 128), F32),
        )
        + tuple(pltpu.HBM(shape, BF16) for shape in slopes),
        in_specs=[smem_spec()] + vmem_specs(6) + far_specs(3),
        out_specs=tuple(far_specs(1) + vmem_specs(2) + far_specs(3)),
        scratch_shapes=[pltpu.VMEM((padded, 3 * LANES), BF16)] * 2
        + [pltpu.VMEM((BLOCK * width, LANES), F32)] * 2
        + weight_scratch(weights)
        + [pltpu.VMEM(pre, F32)] + [pltpu.VMEM(((rows + 1) * width, 128), F32)] * 2
        + [pltpu.VMEM(shape, BF16) for shape in slopes]
        + [pltpu.SemaphoreType.DMA((LAYERS,)), pltpu.SemaphoreType.DMA((LAYERS - 1 + rows // BLOCK,))],
        compiler_params=params(34),
        name="forward_pass",
    )(place, *in_hbm(own), *lon, *lat, operator, *in_hbm(*weights))


LEAD = HALO + 1


def slope_rows(layer, first):
    return first - (layer - HALO + 1)


def edge_kernel(
    place_ref, recv_ref, pred_ref, pred_edge_ref, op_ref, prec_ref, prec_edge_ref,
    d0_far, d1_far, d2_far, w0_far, wm_far, w3_far,
    pulled_far, near_ref, far_ref, s0_ref, s1_ref, s2_ref,
    pulled_ref, pulled_sem, wide_ref, sums_ref, field_a, field_b, buf_a, buf_b, acc_a, acc_b, w0, wm, w3, d_ref, in_sems,
):
    rows, cells, channels = pred_ref.shape[0], pred_ref.shape[2], near_ref.shape[1]
    width = cells + 2 * SIDE
    slots = recv_ref.shape[0] // SLOT
    weights = (w0, wm.at[0], wm.at[1], w3)
    strips = (s0_ref, s1_ref, s2_ref)
    size = HALO * width
    pairs = [(w3_far, w3), (wm_far.at[1], wm.at[1]), (wm_far.at[0], wm.at[0]), (w0_far, w0)]
    for layer, source in ((2, d2_far), (1, d1_far), (0, d0_far)):
        for end in range(2):
            first = layer + 1 - HALO if end == 0 else rows - 1 - layer
            at = slope_rows(layer, first) * width
            pairs.append((source.at[pl.ds(at, size)], d_ref.at[layer, end]))
    loads = copies(pairs, in_sems)
    for load in loads:
        load.start()

    nothing = jnp.zeros((4 * width, 3 * LANES), BF16)
    buf_a[width : 5 * width, :] = nothing
    buf_a[(rows + 5) * width : (rows + 9) * width, :] = nothing
    buf_b[0 : 4 * width, :] = nothing
    buf_b[(rows + 6) * width : (rows + 10) * width, :] = nothing

    wide_ref[0 : slots * SLOT, :] = recv_ref[...].astype(F32)
    sums_ref[...] = jnp.zeros(sums_ref.shape, F32)
    sides = [wide_ref[pl.ds(BANDS + end, slots, stride=SLOT), :] for end in range(2)]
    lane = lax.broadcasted_iota(jnp.int32, (slots, cells), 1).astype(F32)
    own = sides[0][:, BANDS + 1 : BANDS + 2]
    before = sides[0][:, BANDS : BANDS + 1] + rows
    after = sides[1][:, BANDS : BANDS + 1] + 2 * rows
    wanted = jnp.where(lane < rows, own, jnp.where(lane < 2 * rows, before, after))
    least = jnp.where(lane < rows, 0.0, jnp.where(lane < 2 * rows, 1.0 * rows, 2.0 * rows))
    match = (wanted == lane + 1.0) & (wanted > least) & (lane < 3 * rows)
    onehot = jnp.transpose(match.astype(F32))[0 : 3 * rows, :].astype(BF16)
    held = jnp.dot(onehot, jnp.ones((slots, cells), BF16), preferred_element_type=F32)
    own_hot = onehot[0:rows, :]
    for k in range(BANDS):
        part = wide_ref[pl.ds(k, slots, stride=SLOT), :].astype(BF16)
        sums_ref[pl.ds(k, rows, stride=32), :] = jnp.dot(own_hot, part, preferred_element_type=F32)
    nothing = jnp.zeros((SIDE, 128), F32)
    for r in range(rows):
        summed = sums_ref[r * 32 : (r + 1) * 32, :]
        weighted = (summed - held[r : r + 1, :] * pred_ref[r]) * prec_ref[...]
        at = r * width
        value = jnp.dot(
            jnp.transpose(weighted).astype(BF16), op_ref[...], preferred_element_type=F32
        )
        for field, part in ((field_a, value[:, 0:128]), (field_b, value[:, 128:LANES])):
            field[at : at + SIDE, :] = nothing
            field[at + SIDE : at + SIDE + cells, :] = part
            field[at + SIDE + cells : at + width, :] = nothing
    short = op_ref[...].astype(F32)[0:SLOT, :]
    for end, first in ((0, SIDE - EDGE), (1, SIDE + cells)):
        part = onehot[(1 + end) * rows : (2 + end) * rows, :]
        summed = jnp.dot(part, sides[end].astype(BF16), preferred_element_type=F32)
        count = held[(1 + end) * rows : (2 + end) * rows, :]
        weighted = ((summed - count * pred_edge_ref[end]) * prec_edge_ref[...]).astype(BF16)
        for c in range(EDGE):
            above = [jnp.zeros((c * SLOT, LANES), F32)] if c else []
            below = jnp.zeros((128 - (c + 1) * SLOT, LANES), F32)
            picked = jnp.concatenate(above + [short, below], axis=0).astype(BF16)
            value = jnp.dot(weighted, picked, preferred_element_type=F32)
            at = pl.ds(first + c, rows, stride=width)
            field_a[at, :] = value[:, 0:128]
            field_b[at, :] = value[:, 128:LANES]
    for r in range(rows):
        at = slice(r * width, (r + 1) * width)
        row = jnp.concatenate([field_a[at, :], field_b[at, :]], axis=1)[:, 0:channels]
        pulled_ref[r] = row
        if r < HALO or r >= rows - HALO:
            put_shifted(buf_a, r + LEAD, width, row)
    sent = copies(((pulled_ref, pulled_far),), pulled_sem)[0]
    sent.start()

    src, dst = buf_a, buf_b
    for layer in range(LAYERS - 1, -1, -1):
        margin = LAYERS - layer
        tops = (-margin, rows + margin - HALO)
        accs = (acc_a, acc_b)
        loads[LAYERS - 1 - layer].wait()
        for end in range(2):
            value = conv_block(
                src, tops[end] + LEAD - 1, HALO, width, weights[layer], 1 if layer == 0 else 0, True
            )
            accs[end][:, 0 : value.shape[1]] = value
        if layer > 0:
            for end in range(2):
                loads[LAYERS + 2 * (LAYERS - 1 - layer) + end].wait()
                value = accs[end][...] * d_ref[layer - 1, end].astype(F32)
                put_shifted(dst, tops[end] + LEAD, width, value)
                half = size // 2
                kept = value[half:, :] if end == 0 else value[0:half, :]
                strips[layer - 1][end * half : (end + 1) * half, :] = kept.astype(BF16)
        else:
            for i in range(HALO):
                at = slice(i * width + SIDE, i * width + SIDE + cells)
                top = acc_a[at, 0:channels]
                low = acc_b[at, 0:channels]
                near_ref[i] = jnp.transpose(either(place_ref[1], low, top)).astype(BF16)
                far_ref[i] = jnp.transpose(either(place_ref[1], top, low)).astype(BF16)
        src, dst = dst, src
    sent.wait()


def edge_pass(place, recv, pred, pred_edge, slopes, operator, precision, precision_edge, weights, channels):
    rows, cells = pred.shape[0], pred.shape[2]
    width = cells + 2 * SIDE
    padded = (rows + 2 * LEAD) * width
    size = HALO * width
    return pl.pallas_call(
        edge_kernel,
        out_shape=(
            pltpu.HBM((rows, width, channels), F32),
            jax.ShapeDtypeStruct((HALO, channels, cells), BF16),
            jax.ShapeDtypeStruct((HALO, channels, cells), BF16),
        )
        + tuple(pltpu.HBM((size, LANES), BF16) for _ in range(LAYERS - 1)),
        in_specs=[smem_spec()] + vmem_specs(6) + far_specs(6),
        out_specs=tuple(far_specs(1) + vmem_specs(5)),
        scratch_shapes=[
            pltpu.VMEM((rows, width, channels), F32),
            pltpu.SemaphoreType.DMA((1,)),
            pltpu.VMEM((recv.shape[0] + SLOT, recv.shape[1]), F32),
            pltpu.VMEM(((rows + 1) * 32, recv.shape[1]), F32),
            pltpu.VMEM(((rows + 1) * width, 128), F32),
            pltpu.VMEM(((rows + 1) * width, 128), F32),
        ]
        + [pltpu.VMEM((padded, 3 * LANES), BF16)] * 2
        + [pltpu.VMEM((size, LANES), F32)] * 2
        + weight_scratch(weights)
        + [pltpu.VMEM((LAYERS - 1, 2, size, LANES), BF16), pltpu.SemaphoreType.DMA((LAYERS + 6,))],
        compiler_params=params(34),
        name="edge_pass",
    )(place, recv, *in_hbm(pred, pred_edge), operator, precision, precision_edge, *in_hbm(*slopes, *weights))


def inner_kernel(
    scale_ref, pulled_ref, s0_ref, s1_ref, s2_ref,
    pre_far, d0_far, d1_far, d2_far, w0_far, wm_far, w3_far, state_far, noise_far,
    base_ref,
    buf_a, buf_b, acc_a, acc_b, w0, wm, w3, pre_ref, d0, d1, d2, state_ref, noise_ref, in_sems,
):
    rows, width, _ = pulled_ref.shape
    cells = width - 2 * SIDE
    level = jnp.full((1, 128), scale_ref[0], F32)
    inverse = (1.0 / (level * level))[:, 0:1]
    step = jnp.full((1, 128), scale_ref[1], F32)
    spread = jnp.sqrt(2.0 * step)
    weights = (w0, wm.at[0], wm.at[1], w3)
    strips = (s0_ref, s1_ref, s2_ref)
    slopes = (d0, d1, d2)
    pairs = [(w3_far, w3)]
    for layer, source, weight in ((2, d2_far, 1), (1, d1_far, 0), (0, d0_far, None)):
        first = layer + 1
        count = slopes[layer].shape[0]
        pairs.append((source.at[pl.ds(slope_rows(layer, first) * width, count)], slopes[layer]))
        pairs.append((w0_far, w0) if weight is None else (wm_far.at[weight], wm.at[weight]))
    pairs += [(pre_far, pre_ref), (state_far, state_ref), (noise_far, noise_ref)]
    loads = copies(pairs, in_sems)
    for load in loads:
        load.start()

    def fill(r, carry):
        put_shifted(buf_a, r + LEAD, width, pulled_ref[r])
        return carry

    lax.fori_loop(LAYERS - 2, rows - LAYERS + 2, fill, 0)
    loads[0].wait()
    src, dst = buf_a, buf_b
    half = HALO // 2 * width
    for layer in range(LAYERS - 1, -1, -1):
        begin = layer
        count = rows - 2 * layer

        def compute(row, n, src=src, layer=layer, begin=begin):
            return conv_block(
                src, row + begin + LEAD - 1, n, width, weights[layer], 1 if layer == 0 else 0, True
            )

        if layer > 0:
            kept = strips[layer - 1]
            put_shifted(dst, layer - 2 + LEAD, width, kept[0:half, :].astype(F32))
            put_shifted(dst, rows - layer + LEAD, width, kept[half:, :].astype(F32))
            loads[2 * (LAYERS - 1 - layer) + 1].wait()

            def finish(row, n, value, dst=dst, layer=layer, begin=begin):
                slope = slopes[layer - 1][pl.ds(row * width, n * width), :]
                put_shifted(dst, row + begin + LEAD, width, value * slope.astype(F32))

            conv_layer(count, compute, finish, acc_a, acc_b)
            loads[2 * (LAYERS - 1 - layer) + 2].wait()
        else:
            for load in loads[-3:]:
                load.wait()

            def finish(row, n, value):
                for i in range(n):
                    total = pre_ref[row + i] * inverse + pulled_ref[row + i] + value[i * width : (i + 1) * width, :]
                    turned = jnp.transpose(total[SIDE : SIDE + cells, :])
                    r = row + i
                    base_ref[:, r, :] = state_ref[:, r, :] + step * turned + spread * noise_ref[:, r, :]

            conv_layer(count, compute, finish, acc_a, acc_b)
        src, dst = dst, src


def inner_pass(scale, pulled, strips, pre, slopes, weights, state, noise):
    rows, width, _ = pre.shape
    padded = (rows + 2 * LEAD) * width
    kept = [((rows - 2 * (layer + 1)) * width, LANES) for layer in range(LAYERS - 1)]
    return pl.pallas_call(
        inner_kernel,
        out_shape=jax.ShapeDtypeStruct(state.shape, F32),
        in_specs=[smem_spec()] + vmem_specs(4) + far_specs(9),
        out_specs=vmem_specs(1)[0],
        scratch_shapes=[pltpu.VMEM((padded, 3 * LANES), BF16)] * 2
        + [pltpu.VMEM((BLOCK * width, LANES), F32)] * 2
        + weight_scratch(weights)
        + [pltpu.VMEM(pre.shape, F32)]
        + [pltpu.VMEM(shape, BF16) for shape in kept]
        + [pltpu.VMEM(state.shape, F32)] * 2
        + [pltpu.SemaphoreType.DMA((2 * LAYERS + 2,))],
        compiler_params=params(34),
        name="inner_pass",
    )(scale, *in_hbm(pulled, *strips, pre, *slopes, *weights, state, noise))


def final_kernel(place_ref, scale_ref, base_ref, near_ref, far_ref, out_ref):
    rows = base_ref.shape[1]
    step = jnp.full((1, 128), scale_ref[1], F32)
    out_ref[...] = base_ref[...]
    for i in range(HALO):
        near = near_ref[i].astype(F32)
        far = far_ref[i].astype(F32)
        r = rows - HALO + i
        out_ref[:, i, :] = base_ref[:, i, :] + step * either(place_ref[1], far, near)
        out_ref[:, r, :] = base_ref[:, r, :] + step * either(place_ref[1], near, far)


def final_pass(place, scale, base, near, far):
    return pl.pallas_call(
        final_kernel,
        out_shape=jax.ShapeDtypeStruct(base.shape, F32),
        in_specs=[smem_spec(), smem_spec()] + vmem_specs(3),
        out_specs=vmem_specs(1)[0],
        compiler_params=params(8),
        name="final_pass",
    )(place, scale, base, near, far)


def swap_pairs(size, first, wrap):
    pairs = []
    for low in range(first, size if wrap else size - 1, 2):
        high = (low + 1) % size
        pairs += [(low, high), (high, low)]
    return pairs


def swap(axis, wrap, near, far):
    size = lax.axis_size(axis)
    return lax.ppermute(near, axis, swap_pairs(size, 0, wrap)), lax.ppermute(far, axis, swap_pairs(size, 1, wrap))


def pad_to(values, shape):
    return jnp.pad(values, [(0, n - m) for m, n in zip(values.shape, shape)])


def shards(
    state,
    noise,
    first_kernel,
    middle_kernels,
    last_kernel,
    obs_values,
    obs_holder,
    obs_tile,
    obs_operator,
    obs_precision,
    noise_level,
    step_size,
):
    channels, rows, cells = state.shape
    width = cells + 2 * SIDE
    weights = (jnp.transpose(first_kernel, (0, 2, 1)), middle_kernels, last_kernel)
    lon, lat = lax.axis_index("lon"), lax.axis_index("lat")
    bands = lax.axis_size("lat")
    place = jnp.stack([lon % 2 == 0, lat % 2 == 0, lat == 0, lat == bands - 1]).astype(jnp.int32)

    holders = lax.axis_size(("lon", "lat"))
    packed = pack_blocks(obs_holder, obs_tile, obs_values, holders * CAPACITY, bands * CAPACITY)
    own, outer, *edges = turn_state(place, state)
    lon_halo = swap("lon", True, *edges)
    framed = frame_rows(place, outer, *lon_halo, width)
    packed, framed = lax.optimization_barrier((packed, framed))
    lat_halo = swap("lat", False, *framed)
    recv = lax.all_to_all(
        packed.reshape(holders, CAPACITY * SLOT, cells), ("lon", "lat"), split_axis=0, concat_axis=0, tiled=True
    ).reshape(packed.shape)

    operator = pad_to(obs_operator, (32, LANES))
    precision = pad_to(obs_precision[:, None], (32, 1))
    precision_edge = pad_to(jnp.tile(pad_to(obs_precision, (SLOT,)), EDGE)[None, :], (1, 128))
    pre, pred, pred_edge, *slopes = forward_pass(place, own, lon_halo, lat_halo, weights, operator, rows, width)
    pulled, near, far, *strips = edge_pass(
        place, recv, pred, pred_edge, slopes, operator, precision, precision_edge, weights, channels
    )
    near, far = swap("lat", False, near, far)
    scale = jnp.concatenate([noise_level, step_size])
    base = inner_pass(scale, pulled, strips, pre, slopes, weights, state, noise)
    return final_pass(place, scale, base, near, far)


def solution(mesh):
    placed = (
        P(None, "lat", "lon"),
        P(None, "lat", "lon"),
        P(),
        P(),
        P(),
        P(("lon", "lat"), None, None),
        P(("lon", "lat"), None),
        P(("lon", "lat")),
        P(),
        P(),
        P(),
        P(),
    )

    return jax.shard_map(shards, mesh=mesh, in_specs=placed, out_specs=P(None, "lat", "lon"), check_vma=False)
```
